512 devices in a mesh: member: 32 (over z_hi, y, core), tile: 16 (over z_lo, x).
Axes of the slice: x: 4, y: 8, z: 8 (z_hi: 2, z_lo: 4; z = z_hi * 4 + z_lo), core: 2. Of those that a mesh axis runs over, the one named last changes fastest.
Arguments:
- perturbations: bfloat16 [256, 2, 5, 8, 32, 2048], P('member', None, None, None, None, 'tile'), may hold values from -6 to 6
- gradient_store: float32 [2, 5, 8, 32, 2048], P(None, None, None, 'member', 'tile'), may hold values from -6 to 6
- diffusivity: float32 [8, 32, 2048], P(None, None, 'tile'), may hold values from 0.2 to 0.4
- slab_owner: int32 [32], replicated, may hold values from 0 to 31, each once
Outputs:
- increment_store: float32 [2, 5, 8, 32, 2048], P(None, None, None, 'member', 'tile')
The draws below stay inside these ranges and needn't reach their ends.
Inputs may be any that keep to these rules, and one draw needn't show every extreme that they name: `slab_owner`: each member index holds exactly one slab.
All inputs are finite; a program needn't handle non-finite values.
Results may differ from the reference program's by a relative error of at most 0.0003.
Values sent between devices are 32-bit elements; how exact they have to be, the bound alone decides.
A program may use at most 128 MiB of HBM per device.

```python
import math
import jax
import jax.numpy as jnp
from jax import lax

SLOTS = 2
VARS = 5
NZ = 8
SWEEPS = 10
YSLAB = 1
MEMBERS = 256
NX = 2048
NY = 32
N_MEMBER = 32


def strengthened(array, own_key, source, target, parts, factor):
    owner, partner = [(jnp.arange(array.shape[dim]) // (array.shape[dim] // parts)).reshape([-1 if axis == dim else 1 for axis in range(array.ndim)]) for dim in (source, target)]
    chosen = jax.random.permutation(own_key, parts)[partner]
    strong = (owner == chosen) | (owner == (partner + parts // 2) % parts)
    return jnp.where(strong, factor * array, array)


def level_of(own_key, extent, split, smallest, largest):
    gain, own = 1.0, jax.random.fold_in(own_key, 6)
    for position, blocks in split:
        heights = jnp.exp(jax.random.uniform(jax.random.fold_in(own, position), (blocks,), jnp.float32, smallest / len(split), largest / len(split)))
        gain = gain * jnp.repeat(heights, extent[position] // blocks).reshape([-1 if axis == position else 1 for axis in range(len(extent))])
    return gain


def normal_values(stream_key, extent, spread, most, pieces=(), kind=jnp.bfloat16):
    entries = jax.random.normal(stream_key, extent, jnp.float32) * spread
    if len(pieces) > 0:
        entries = level_of(stream_key, extent, pieces, -0.22, 0.18) * entries
    return jnp.clip(entries, min=-most, max=most).astype(kind)


def bell_draw_with(key, extent, scale, reach, cuts, heavy, kind=jnp.bfloat16):
    drawn = scale * jax.random.normal(key, extent, jnp.float32)
    if cuts:
        drawn = drawn * level_of(key, extent, cuts, -0.22, 0.18)
    return jnp.clip(strengthened(drawn, jax.random.fold_in(key, 3), *heavy), -reach, reach).astype(kind)


def setup_inputs(seed: int = 0) -> dict:
    key_of = jax.random.split(jax.random.key(seed), 5)
    return {
        "perturbations": bell_draw_with(key_of[0], (MEMBERS, SLOTS, VARS, NZ, NY, NX), 1.0, 6.0, ((0, 32), (5, 16)), (0, 4, 32, 2.75)),
        "gradient_store": normal_values(key_of[1], (SLOTS, VARS, NZ, NY, NX), 1.0, 6.0, ((3, 32), (4, 16)), jnp.float32),
        "diffusivity": jnp.clip(jnp.exp(math.log(0.4) - 0.6931472 * jax.random.uniform(key_of[2], (NZ, NY, NX), jnp.float32) ** level_of(key_of[2], (NZ, NY, NX), ((2, 16),), -0.2, 0.2)), 0.2, 0.4),
        "slab_owner": jax.random.permutation(key_of[3], N_MEMBER).astype(jnp.int32),
    }


def neighbours(grid_field):
    count = grid_field.ndim
    widths_y = [(0, 0)] * (count - 2) + [(1, 1), (0, 0)]
    widths_z = [(0, 0)] * (count - 3) + [(1, 1), (0, 0), (0, 0)]
    padded_y = jnp.pad(grid_field, widths_y)
    padded_z = jnp.pad(grid_field, widths_z)
    return padded_y[..., :-2, :] + padded_y[..., 2:, :] + padded_z[..., :-2, :, :] + padded_z[..., 2:, :, :]


def diffuse(values, coefficient):
    scaled = coefficient * values
    centre = values[..., 1:-1]
    coeff_mid = coefficient[..., 1:-1]
    scaled_mid = scaled[..., 1:-1]
    inflow = scaled[..., :-2] + scaled[..., 2:] + neighbours(scaled_mid)
    outflow = coefficient[..., :-2] + coefficient[..., 2:] + neighbours(coeff_mid)
    return centre + coeff_mid * (inflow - outflow * centre)


def block_rows(slab_owner, slab_rows):
    offsets = jnp.arange(slab_rows, dtype=jnp.int32)
    return (slab_owner.astype(jnp.int32)[:, None] * slab_rows + offsets[None, :]).reshape(-1)


def reference(perturbations, gradient_store, diffusivity, slab_owner):
    true_rows = block_rows(slab_owner, YSLAB)
    gradient = jnp.take(gradient_store, true_rows, axis=3)
    coeff_ext = jnp.pad(diffusivity, ((0, 0), (0, 0), (1, 1)))

    def one_sweep(sweep_index, field_state):
        return diffuse(jnp.pad(field_state, ((0, 0), (0, 0), (1, 1))), coeff_ext)

    def member_step(running, member):
        member_float = member.astype(jnp.float32)
        weighted = jnp.sum(member_float * gradient, axis=(0, 1))
        local_field = lax.fori_loop(0, SWEEPS, one_sweep, weighted)
        return running + member_float * local_field[None, None], None

    start_sum = jnp.zeros((SLOTS, VARS, NZ, NY, NX), jnp.float32)
    running, unused = lax.scan(member_step, start_sum, perturbations)
    increment = running * (1.0 / (MEMBERS - 1))
    store_rows = block_rows(jnp.argsort(slab_owner).astype(jnp.int32), YSLAB)
    return jnp.take(increment, store_rows, axis=3)
```

```python
import functools

import jax
import jax.numpy as jnp
from jax import lax
from jax.experimental import pallas as pl
from jax.experimental.pallas import tpu as pltpu
from jax.sharding import PartitionSpec as P

MESH = pl.DeviceIdType.MESH
F32 = jnp.float32
SWEEPS = 10
SV = 10
M = 8
NZ = 8
NY = 32
RING = 8
ROW = NZ * M
VMEM = pl.BlockSpec(memory_space=pltpu.VMEM)
SMEM = pl.BlockSpec(memory_space=pltpu.SMEM)
LIMIT = 60 * 1024 * 1024


def lanes(rows):
    return lax.broadcasted_iota(jnp.int32, (rows, 128), 1)


def roll(value, shift):
    shift = shift % 128
    return value if shift == 0 else pltpu.roll(value, shift, 1)


def up(row, above):
    cut = row.shape[0] - M
    return jnp.concatenate([row[:cut] + above[M:], row[cut:]], axis=0)


def six(p0, pu, cur, nxt):
    u = up(nxt, cur)
    four = u + jnp.concatenate([p0, pu[: ROW - M]], axis=0)
    return four + (roll(cur, 1) + roll(cur, 127)), u


def main_pass(src, emit, unroll=2):
    cur = src[pl.ds(0, ROW), :]

    def body(y, carry):
        p0, pu, cur = carry
        nxt = src[pl.ds(pl.multiple_of((y + 1) * ROW, ROW), ROW), :]
        total, u = six(p0, pu, cur, nxt)
        emit(pl.ds(pl.multiple_of(y * ROW, ROW), ROW), cur, total)
        return cur[:M], u, nxt

    lax.fori_loop(0, NY, body, (jnp.zeros((M, 128), F32), cur, cur), unroll=unroll)


def strip_pass(src, lo, hi, emit):
    first, last = src[pl.ds(0, ROW), :], src[pl.ds(7 * ROW, ROW), :]
    prev = jnp.where(lo, 0.0, roll(last, 32))
    beyond = jnp.where(hi, 0.0, roll(first, 96))
    p0, pu, cur = prev[:M], up(first, prev), first
    for y in range(8):
        nxt = src[pl.ds((y + 1) * ROW, ROW), :] if y < 7 else beyond
        total, u = six(p0, pu, cur, nxt)
        emit(pl.ds(y * ROW, ROW), cur, total)
        p0, pu, cur = cur[:M], u, nxt


def strip_masks():
    lane = lanes(ROW)
    left = ((lane >= 118) | (lane < 22), (lane >= 86) & (lane < 118))
    right = ((lane >= 106) | (lane < 10), (lane >= 74) & (lane < 106))
    return left, right


def coefficients(src, dst_a, dst_q, strip=None):
    def emit(rows, cur, total):
        dst_a[rows, :] = 1.0 - cur * total
        dst_q[rows, :] = cur * cur

    if strip is None:
        main_pass(src, emit)
    else:
        strip_pass(src, *strip, emit)


def stepper(dst, a, q):
    def emit(rows, cur, total):
        dst[rows, :] = a[rows, :] * cur + q[rows, :] * total

    return emit


def k_strips(k_ref, left_ref, right_ref):
    region = lanes(8) // 32
    for z in range(NZ):
        turned = [roll(k_ref[z, pl.ds(8 * h, 8), :], 32 * h) for h in range(4)]
        left, right = turned[0], turned[0]
        for h in range(1, 4):
            left = jnp.where(region == h, turned[h], left)
            right = jnp.where(region == h - 1, turned[h], right)
        left_ref[z] = left
        right_ref[z] = right


def spread(value_of, dst, blocks, pad=True):
    def body(z, carry):
        for b in range(blocks):
            value = value_of(z, b)
            for m in range(M):
                dst[pl.ds(b * 8 * ROW + z * M + m, 8, stride=ROW), :] = value
        return carry

    lax.fori_loop(0, NZ, body, 0)


def prepare_kernel(k_ref, kl_ref, kr_ref, a_ref, q_ref, kb):
    k_strips(k_ref, kl_ref, kr_ref)
    kb[pl.ds(NY * ROW, ROW), :] = jnp.zeros((ROW, 128), F32)
    spread(lambda z, b: k_ref[z, pl.ds(8 * b, 8), :], kb, 4)
    coefficients(kb, a_ref, q_ref)


def strip_prepare(kl_ref, kr_ref, hl_ref, hr_ref, al, ql, ar, qr, kb):
    lane = lanes(8) % 32
    left, right = strip_masks()
    spread(lambda z, b: jnp.where(lane >= 22, hl_ref[z], kl_ref[z]), kb, 1)
    coefficients(kb, al, ql, left)
    spread(lambda z, b: jnp.where(lane < 10, hr_ref[z], kr_ref[z]), kb, 1)
    coefficients(kb, ar, qr, right)


def member(zh, y, c):
    return {"member": (zh * RING + lax.rem(y + RING, RING)) * 2 + c}


def here():
    i = lax.axis_index("member")
    return i // (2 * RING), lax.rem(i // 2, RING), lax.rem(i, 2)


def greet(targets, conditional=()):
    barrier = pltpu.get_barrier_semaphore()
    count = len(targets)
    for target in targets:
        pl.semaphore_signal(barrier, inc=1, device_id=target, device_id_type=MESH)
    for condition, target in conditional:
        @pl.when(condition)
        def _():
            pl.semaphore_signal(barrier, inc=1, device_id=target, device_id_type=MESH)

        count = count + jnp.where(condition, 1, 0)
    pl.semaphore_wait(barrier, count)


def copy_to(src, dst, send, recv, target):
    return pltpu.make_async_remote_copy(
        src_ref=src, dst_ref=dst, send_sem=send, recv_sem=recv, device_id=target, device_id_type=MESH
    )


def tile_links():
    t, n = lax.axis_index("tile"), lax.axis_size("tile")
    return (t > 0, {"tile": lax.rem(t + n - 1, n)}), (t < n - 1, {"tile": lax.rem(t + 1, n)})


def halo_start(to_left, to_right, from_left, from_right, send, recv):
    (has_left, left), (has_right, right) = tile_links()
    rightward = copy_to(to_right, from_left, send.at[0], recv.at[0], right)
    leftward = copy_to(to_left, from_right, send.at[1], recv.at[1], left)

    @pl.when(has_right)
    def _():
        rightward.start()

    @pl.when(has_left)
    def _():
        leftward.start()

    @pl.when(jnp.logical_not(has_left))
    def _():
        from_left[...] = jnp.zeros(from_left.shape, F32)

    @pl.when(jnp.logical_not(has_right))
    def _():
        from_right[...] = jnp.zeros(from_right.shape, F32)

    def finish():
        @pl.when(has_right)
        def _():
            rightward.wait_send()
            leftward.wait_recv()

        @pl.when(has_left)
        def _():
            leftward.wait_send()
            rightward.wait_recv()

    return finish


def gather_kernel(grad, kl, kr, full, hl, hr, y_send, y_recv, p_send, p_recv, z_sem, local_sem, h_send, h_recv):
    zh, y, c = here()
    near = [member(zh, y + d, c) for d in (1, 2, -1, -2)]
    anti, pair = member(1 - zh, y, c), member(zh, y, 1 - c)
    greet(near + [anti, pair], tile_links())

    half = SV * NZ // 2
    lower, upper = pl.ds(0, half), pl.ds(half, half)
    waits = []

    def slot(side, d, core=c):
        z = zh if side == 0 else 1 - zh
        return member(z, y + d, core)["member"]

    mine = pltpu.make_async_copy(grad, full.at[slot(0, 0)], local_sem)
    mine.start()

    def y_copy(side, kind, source_block=None):
        d, to, rows = {
            0: (0, 1, None), 1: (0, 2, None), 2: (0, -1, None), 3: (0, -2, None),
            4: (-2, 1, None), 5: (-2, 2, lower), 6: (2, -1, None), 7: (2, -2, upper),
        }[kind]
        place = full.at[slot(side, d)] if rows is None else full.at[slot(side, d), rows]
        source = place if source_block is None else source_block
        return copy_to(source, place, y_send.at[side, kind], y_recv.at[side, kind], near[{1: 0, 2: 1, -1: 2, -2: 3}[to]])

    def y_start(side, kind, source_block=None):
        op = y_copy(side, kind, source_block)
        op.start()
        waits.append(op)

    def y_arrived(side, kind):
        y_copy(side, kind).wait_recv()

    def pass_on(number, place, source=None):
        op = copy_to(place if source is None else source, place, p_send.at[number], p_recv.at[number], pair)
        op.start()
        waits.append(op)

    cross = copy_to(grad, full.at[slot(0, 0)], z_sem.at[0], z_sem.at[1], anti)
    cross.start()
    for kind in (1, 3, 0, 2):
        y_start(0, kind, grad)
    pass_on(0, full.at[slot(0, 0)], grad)
    halos = halo_start(kl, kr, hl, hr, h_send, h_recv)

    def arrivals(side, kinds):
        for kind in kinds:
            y_arrived(side, kind)
            d, rows = {
                0: (-1, None), 1: (-2, None), 2: (1, None), 3: (2, None),
                4: (-3, None), 5: (-4, lower), 6: (3, None), 7: (4, upper),
            }[kind]
            if kind == 1:
                y_start(side, 5)
                y_start(side, 4)
            if kind == 3:
                y_start(side, 7)
                y_start(side, 6)
            place = full.at[slot(side, d)] if rows is None else full.at[slot(side, d), rows]
            pass_on(1 + side * 9 + kind, place)

    arrivals(0, (0, 2, 1, 3))
    cross.wait_recv()
    for kind in (1, 3, 0, 2):
        y_start(1, kind)
    pass_on(9, full.at[slot(1, 0)])
    arrivals(0, (4, 6, 5, 7))
    arrivals(1, (0, 2, 1, 3, 4, 6, 5, 7))

    halos()
    mine.wait()
    cross.wait_send()
    for op in waits:
        op.wait_send()
    for number in range(18):
        side, kind = divmod(number - 1, 9) if number else (0, None)
        if number in (0, 9):
            place = full.at[slot(0 if number == 0 else 1, 0, 1 - c)]
        else:
            d, rows = {
                0: (-1, None), 1: (-2, None), 2: (1, None), 3: (2, None),
                4: (-3, None), 5: (-4, lower), 6: (3, None), 7: (4, upper),
            }[kind]
            place = full.at[slot(side, d, 1 - c)]
            place = place if rows is None else place.at[rows]
        copy_to(place, place, p_send.at[number], p_recv.at[number], pair).wait_recv()


def weigh_kernel(owner, full, pert, k_ref, state, pad_rows, gt):
    state[pl.ds(NY * ROW, ROW), :] = jnp.zeros((ROW, 128), F32)

    def regroup(y, carry):
        o = owner[y]
        for sv in range(SV):
            gt[pl.ds(sv * NZ * NY + y, NZ, stride=NY), :] = full[o, pl.ds(sv * NZ, NZ), :]
        return carry

    lax.fori_loop(0, NY, regroup, 0)

    def body(i, carry):
        z, b = i // 2, lax.rem(i, 2)
        y0 = pl.multiple_of(b * 16, 16)
        grads = [gt[pl.ds(pl.multiple_of(sv * NZ * NY + z * NY + y0, 16), 16), :] for sv in range(SV)]
        k = k_ref[z, pl.ds(y0, 16), :]
        for m in range(M):
            total = None
            for sv in range(SV):
                term = pert[m, sv, z, pl.ds(y0, 16), :].astype(F32) * grads[sv]
                total = term if total is None else total + term
            total = total * k
            for part in range(2):
                start = (y0 + 8 * part) * ROW + z * M + m
                state[pl.ds(start, 8, stride=ROW), :] = total[8 * part : 8 * part + 8]
        return carry

    lax.fori_loop(0, 2 * NZ, body, 0)


def cut_strips(state, vl, vr):
    region = lanes(ROW) // 32

    def body(y, carry):
        turned = [roll(state[pl.ds(pl.multiple_of((8 * h + y) * ROW, ROW), ROW), :], 32 * h) for h in range(4)]
        left, right = turned[0], turned[0]
        for h in range(1, 4):
            left = jnp.where(region == h, turned[h], left)
            right = jnp.where(region == h - 1, turned[h], right)
        rows = pl.ds(pl.multiple_of(y * ROW, ROW), ROW)
        vl[rows, :] = left
        vr[rows, :] = right
        return carry

    lax.fori_loop(0, 8, body, 0)


def evens(row, odd):
    return jnp.concatenate([row[M * (2 * i + odd) : M * (2 * i + odd + 1)] for i in range(4)], axis=0)


def pack_strips(vl, vr, to_left, to_right):
    lane = lanes(ROW // 2) % 32

    def body(y, carry):
        rows = pl.ds(pl.multiple_of(y * ROW, ROW), ROW)
        out = pl.ds(pl.multiple_of(y * ROW // 2, ROW // 2), ROW // 2)
        right, left = vr[rows, :], vl[rows, :]
        to_right[out, :] = jnp.where(lane >= 22, evens(right, 0), roll(evens(right, 1), 118))
        to_left[out, :] = jnp.where(lane < 10, evens(left, 0), roll(evens(left, 1), 10))
        return carry

    lax.fori_loop(0, 8, body, 0)


def unpack_strips(from_left, from_right, vl, vr):
    lane = lanes(ROW) % 32

    def mixed(even, odd):
        return jnp.concatenate([part[M * i : M * i + M] for i in range(4) for part in (even, odd)], axis=0)

    def body(y, carry):
        rows = pl.ds(pl.multiple_of(y * ROW, ROW), ROW)
        packed = pl.ds(pl.multiple_of(y * ROW // 2, ROW // 2), ROW // 2)
        left, right = from_left[packed, :], from_right[packed, :]
        vl[rows, :] = jnp.where(lane >= 22, mixed(left, roll(left, 10)), vl[rows, :])
        vr[rows, :] = jnp.where(lane < 10, mixed(right, roll(right, 118)), vr[rows, :])
        return carry

    lax.fori_loop(0, 8, body, 0)


def halo_kernel(to_left, to_right, from_left, from_right, send, recv):
    greet([], tile_links())
    halo_start(to_left, to_right, from_left, from_right, send, recv)()


def cut_kernel(state, vl, vr, to_left, to_right):
    cut_strips(state, vl, vr)
    pack_strips(vl, vr, to_left, to_right)


def merge_strips(state, vl, vr):
    lane = lanes(ROW)
    inner = (lane >= 10) & (lane < 118)

    def body(y, carry):
        rows = pl.ds(pl.multiple_of(y * ROW, ROW), ROW)
        edge = jnp.where(lane % 32 < 10, vl[rows, :], vr[rows, :])
        for h in range(4):
            place = pl.ds(pl.multiple_of((8 * h + y) * ROW, ROW), ROW)
            state[place, :] = jnp.where(inner, state[place, :], roll(edge, -32 * h))
        return carry

    lax.fori_loop(0, 8, body, 0)


def second_pass(pert, k_ref, state, inc, norm):
    def body(i, carry):
        z, b = i // 2, lax.rem(i, 2)
        y0 = pl.multiple_of(b * 16, 16)
        factor = norm / k_ref[z, pl.ds(y0, 16), :]
        local = []
        for m in range(M):
            starts = [(y0 + 8 * part) * ROW + z * M + m for part in range(2)]
            local.append(jnp.concatenate([state[pl.ds(s, 8, stride=ROW), :] for s in starts], axis=0))
        for sv in range(SV):
            total = None
            for m in range(M):
                term = pert[m, sv, z, pl.ds(y0, 16), :].astype(F32) * local[m]
                total = term if total is None else total + term
            total = total * factor
            for part in range(2):
                start = (y0 + 8 * part) * SV * NZ + sv * NZ + z
                inc[pl.ds(start, 8, stride=SV * NZ), :] = total[8 * part : 8 * part + 8]
        return carry

    lax.fori_loop(0, 2 * NZ, body, 0)


def sweep_kernel(slab_of, pert, k_ref, a, q, kl, kr, hl, hr, state0, vl0, vr0, from_left, from_right, out,
                 s0, s1, l0, l1, r0, r1, al, ql, ar, qr, kb, inc, *, norm):
    strip_prepare(kl, kr, hl, hr, al, ql, ar, qr, kb)
    left, right = strip_masks()
    s0[...] = state0[...]
    l0[...] = vl0[...]
    r0[...] = vr0[...]
    s1[pl.ds(NY * ROW, ROW), :] = jnp.zeros((ROW, 128), F32)
    unpack_strips(from_left, from_right, l0, r0)

    def two(i, carry):
        main_pass(s0, stepper(s1, a, q))
        main_pass(s1, stepper(s0, a, q))
        strip_pass(l0, *left, stepper(l1, al, ql))
        strip_pass(r0, *right, stepper(r1, ar, qr))
        strip_pass(l1, *left, stepper(l0, al, ql))
        strip_pass(r1, *right, stepper(r0, ar, qr))
        return carry

    lax.fori_loop(0, SWEEPS // 2, two, 0)
    merge_strips(s0, l0, r0)
    second_pass(pert, k_ref, s0, inc, norm)
    core = lax.rem(lax.axis_index("member"), 2)

    def order(d, carry):
        for other in range(2):
            row = slab_of[2 * d + (core if other == 0 else 1 - core)]
            out[other, d] = inc[pl.ds(pl.multiple_of(row * SV * NZ, SV * NZ), SV * NZ), :]
        return carry

    lax.fori_loop(0, 2 * RING, order, 0)


def reduce_kernel(sums, out, total, other, step_buf, z_buf, p_send, p_recv, y_send, y_recv, z_sem):
    zh, y, c = here()
    up_to, down_to = member(zh, y + 1, c), member(zh, y - 1, c)
    anti, pair = member(1 - zh, y, c), member(zh, y, 1 - c)
    greet([up_to, down_to, anti, pair])
    half = SV * NZ // 2
    lower, upper = pl.ds(0, half), pl.ds(half, half)
    waits = []

    def block(side, d):
        return (zh if side == 0 else 1 - zh) * RING + lax.rem(y + d + RING, RING)

    order = (4, 3, -3, 2, -2, 1, -1, 0)
    pair_ops = {}
    for n, d in enumerate(order):
        for side in (1, 0):
            b = block(side, d)
            op = copy_to(sums.at[1, b], other.at[b], p_send.at[side, n], p_recv.at[side, n], pair)
            op.start()
            waits.append(op)
            pair_ops[side, d] = op

    def paired(d):
        for side in (1, 0):
            pair_ops[side, d].wait_recv()
            b = block(side, d)
            total[b] = sums[0, b] + other[b]

    def ring(side, direction, k):
        b = block(side, direction * (5 - k))
        rows = (lower if direction > 0 else upper) if k == 1 else pl.ds(0, SV * NZ)
        way = 0 if direction > 0 else 1
        return copy_to(
            total.at[b, rows], step_buf.at[side, way, k - 1, rows], y_send.at[side, way, k - 1],
            y_recv.at[side, way, k - 1], up_to if direction > 0 else down_to,
        )

    paired(4)
    for side in (1, 0):
        for direction in (1, -1):
            op = ring(side, direction, 1)
            op.start()
            waits.append(op)
    for k in (2, 3, 4, 5):
        paired(5 - k)
        if k < 5:
            paired(k - 5)
        for side in (1, 0):
            for direction in (1, -1):
                way = 0 if direction > 0 else 1
                ring(side, direction, k - 1).wait_recv()
                b = block(side, direction * (5 - k))
                if k == 2:
                    rows = lower if direction > 0 else upper
                    total[b, rows, :] += step_buf[side, way, 0, rows, :]
                else:
                    total[b] += step_buf[side, way, k - 2]
                if k < 5:
                    op = ring(side, direction, k)
                    op.start()
                    waits.append(op)
            if k == 5 and side == 1:
                cross = copy_to(total.at[block(1, 0)], z_buf, z_sem.at[0], z_sem.at[1], anti)
                cross.start()
    cross.wait()
    out[...] = total[block(0, 0)] + z_buf[...]
    for op in waits:
        op.wait_send()


def params(collective=None):
    if collective is None:
        return pltpu.CompilerParams(vmem_limit_bytes=LIMIT)
    return pltpu.CompilerParams(vmem_limit_bytes=LIMIT, collective_id=collective, has_side_effects=True)


def f32(*shape):
    return jax.ShapeDtypeStruct(shape, F32)


def call(kernel, outs, ins, scratch=(), collective=None):
    return pl.pallas_call(
        kernel,
        out_shape=outs,
        in_specs=ins,
        out_specs=[VMEM] * len(outs),
        scratch_shapes=list(scratch),
        compiler_params=params(collective),
    )


def body(perturbations, gradient_store, diffusivity, slab_owner):
    members = perturbations.shape[0] * lax.axis_size("member")
    pert = perturbations.reshape(M, SV, NZ, NY, 128)
    grad = gradient_store.reshape(SV * NZ, 128)
    own = jnp.arange(NY, dtype=jnp.int32)
    slab_of = jnp.sum(jnp.where(slab_owner[None, :] == own[:, None], own[None, :], 0), axis=1)
    dma, scr = pltpu.SemaphoreType.DMA, pltpu.VMEM
    big, strip = (NY * ROW, 128), (8 * ROW, 128)
    state_shape, packed = ((NY + 1) * ROW, 128), (4 * ROW, 128)

    kl, kr, a, q = call(
        prepare_kernel, [f32(NZ, 8, 128)] * 2 + [f32(*big)] * 2, [VMEM], [scr(state_shape, F32)]
    )(diffusivity)
    full, hl, hr = call(
        gather_kernel, [f32(2 * 2 * RING, SV * NZ, 128), f32(NZ, 8, 128), f32(NZ, 8, 128)], [VMEM] * 3,
        [dma((2, 8)), dma((2, 8)), dma((19,)), dma((19,)), dma((2,)), dma, dma((2,)), dma((2,))], 0,
    )(grad, kl, kr)
    state, unused = call(
        weigh_kernel, [f32(*state_shape), f32(8, 128)], [SMEM, VMEM, VMEM, VMEM], [scr((SV * NZ * NY, 128), F32)]
    )(slab_owner, full, pert, diffusivity)
    vl, vr, to_left, to_right = call(cut_kernel, [f32(*strip)] * 2 + [f32(*packed)] * 2, [VMEM])(state)
    from_left, from_right = call(halo_kernel, [f32(*packed)] * 2, [VMEM] * 2, [dma((2,)), dma((2,))], 1)(to_left, to_right)
    (sums,) = call(
        functools.partial(sweep_kernel, norm=1.0 / (members - 1)),
        [f32(2, 2 * RING, SV * NZ, 128)],
        [SMEM] + [VMEM] * 13,
        [scr(state_shape, F32)] * 2 + [scr(strip, F32)] * 9 + [scr((NY * SV * NZ, 128), F32)],
    )(slab_of, pert, diffusivity, a, q, kl, kr, hl, hr, state, vl, vr, from_left, from_right)
    (out,) = call(
        reduce_kernel, [f32(SV * NZ, 128)], [VMEM],
        [scr((2 * RING, SV * NZ, 128), F32)] * 2 + [scr((2, 2, 4, SV * NZ, 128), F32), scr((SV * NZ, 128), F32)]
        + [dma((2, 8)), dma((2, 8)), dma((2, 2, 4)), dma((2, 2, 4)), dma((2,))], 2,
    )(sums)
    return out.reshape(gradient_store.shape)


def solution(mesh):
    in_specs = (
        P("member", None, None, None, None, "tile"),
        P(None, None, None, "member", "tile"),
        P(None, None, "tile"),
        P(),
    )
    out_specs = P(None, None, None, "member", "tile")
    return jax.shard_map(body, mesh=mesh, in_specs=in_specs, out_specs=out_specs, check_vma=False)
```

```python
import functools

import jax
import jax.numpy as jnp
from jax import lax
from jax.experimental import pallas as pl
from jax.experimental.pallas import tpu as pltpu
from jax.sharding import PartitionSpec as P

MESH = pl.DeviceIdType.MESH
F32 = jnp.float32
SWEEPS = 10
SV = 10
M = 8
NZ = 8
NY = 32
RING = 8
ROW = NZ * M
VMEM = pl.BlockSpec(memory_space=pltpu.VMEM)
SMEM = pl.BlockSpec(memory_space=pltpu.SMEM)
LIMIT = 60 * 1024 * 1024
UNROLL = 2


def lanes(rows):
    return lax.broadcasted_iota(jnp.int32, (rows, 128), 1)


def roll(value, shift):
    shift = shift % 128
    return value if shift == 0 else pltpu.roll(value, shift, 1)


def up(row, above):
    cut = row.shape[0] - M
    return jnp.concatenate([row[:cut] + above[M:], row[cut:]], axis=0)


def sideways(row):
    return roll(row, 1) + roll(row, 127)


def row_at(y):
    return pl.ds(y * ROW if isinstance(y, int) else pl.multiple_of(y * ROW, ROW), ROW)


def rows_pass(src, count, first, p0, pu, emit, unroll):
    def body(y, carry):
        p0, pu, cur, side = carry
        nxt = src[row_at(y + 1), :]
        beside = sideways(nxt)
        u = up(nxt, cur)
        four = u + jnp.concatenate([p0, pu[: ROW - M]], axis=0)
        emit(row_at(y), cur, four + side)
        return cur[:M], u, nxt, beside

    lax.fori_loop(0, count, body, (p0, pu, first, sideways(first)), unroll=unroll)


def main_pass(src, emit, unroll=UNROLL):
    first = src[row_at(0), :]
    rows_pass(src, NY, first, jnp.zeros((M, 128), F32), first, emit, unroll)


def strip_pass(src, lo, hi, emit, unroll=UNROLL):
    first, last = src[row_at(0), :], src[row_at(7), :]
    prev = jnp.where(lo, 0.0, roll(last, 32))
    src[row_at(8), :] = jnp.where(hi, 0.0, roll(first, 96))
    rows_pass(src, 8, first, prev[:M], up(first, prev), emit, unroll)


def strip_masks():
    lane = lanes(ROW)
    left = ((lane >= 118) | (lane < 22), (lane >= 86) & (lane < 118))
    right = ((lane >= 106) | (lane < 10), (lane >= 74) & (lane < 106))
    return left, right


def coefficients(src, dst_a, dst_q, strip=None):
    def emit(rows, cur, total):
        dst_a[rows, :] = 1.0 - cur * total
        dst_q[rows, :] = cur * cur

    if strip is None:
        main_pass(src, emit)
    else:
        strip_pass(src, *strip, emit)


def stepper(dst, a, q):
    def emit(rows, cur, total):
        dst[rows, :] = a[rows, :] * cur + q[rows, :] * total

    return emit


def k_strips(k_ref, left_ref, right_ref):
    region = lanes(8) // 32
    for z in range(NZ):
        turned = [roll(k_ref[z, pl.ds(8 * h, 8), :], 32 * h) for h in range(4)]
        left, right = turned[0], turned[0]
        for h in range(1, 4):
            left = jnp.where(region == h, turned[h], left)
            right = jnp.where(region == h - 1, turned[h], right)
        left_ref[z] = left
        right_ref[z] = right


def spread(value_of, dst, blocks, pad=True):
    def body(z, carry):
        for b in range(blocks):
            value = value_of(z, b)
            for m in range(M):
                dst[pl.ds(b * 8 * ROW + z * M + m, 8, stride=ROW), :] = value
        return carry

    lax.fori_loop(0, NZ, body, 0)


def strip_prepare(kl_ref, kr_ref, hl_ref, hr_ref, al, ql, ar, qr, kb):
    lane = lanes(8) % 32
    left, right = strip_masks()
    spread(lambda z, b: jnp.where(lane >= 22, hl_ref[z], kl_ref[z]), kb, 1)
    coefficients(kb, al, ql, left)
    spread(lambda z, b: jnp.where(lane < 10, hr_ref[z], kr_ref[z]), kb, 1)
    coefficients(kb, ar, qr, right)


def member(zh, y, c):
    return {"member": (zh * RING + lax.rem(y + RING, RING)) * 2 + c}


def here():
    i = lax.axis_index("member")
    return i // (2 * RING), lax.rem(i // 2, RING), lax.rem(i, 2)


def greet(targets, conditional=()):
    barrier = pltpu.get_barrier_semaphore()
    count = len(targets)
    for target in targets:
        pl.semaphore_signal(barrier, inc=1, device_id=target, device_id_type=MESH)
    for condition, target in conditional:
        @pl.when(condition)
        def _():
            pl.semaphore_signal(barrier, inc=1, device_id=target, device_id_type=MESH)

        count = count + jnp.where(condition, 1, 0)
    pl.semaphore_wait(barrier, count)


def copy_to(src, dst, send, recv, target):
    return pltpu.make_async_remote_copy(
        src_ref=src, dst_ref=dst, send_sem=send, recv_sem=recv, device_id=target, device_id_type=MESH
    )


def tile_links():
    t, n = lax.axis_index("tile"), lax.axis_size("tile")
    return (t > 0, {"tile": lax.rem(t + n - 1, n)}), (t < n - 1, {"tile": lax.rem(t + 1, n)})


def halo_start(to_left, to_right, from_left, from_right, send, recv):
    (has_left, left), (has_right, right) = tile_links()
    rightward = copy_to(to_right, from_left, send.at[0], recv.at[0], right)
    leftward = copy_to(to_left, from_right, send.at[1], recv.at[1], left)

    @pl.when(has_right)
    def _():
        rightward.start()

    @pl.when(has_left)
    def _():
        leftward.start()

    @pl.when(jnp.logical_not(has_left))
    def _():
        from_left[...] = jnp.zeros(from_left.shape, F32)

    @pl.when(jnp.logical_not(has_right))
    def _():
        from_right[...] = jnp.zeros(from_right.shape, F32)

    def finish():
        @pl.when(has_right)
        def _():
            rightward.wait_send()
            leftward.wait_recv()

        @pl.when(has_left)
        def _():
            leftward.wait_send()
            rightward.wait_recv()

    return finish


KINDS = {
    0: (0, 1, 0), 1: (0, 2, 0), 2: (0, -1, 0), 3: (0, -2, 0),
    4: (-2, 1, 0), 5: (-2, 2, 1), 6: (2, -1, 0), 7: (2, -2, 2),
}


def halved(ref, part):
    half = SV * NZ // 2
    return ref if part == 0 else ref.at[pl.ds(0 if part == 1 else half, half)]


def gather(grad, full, near, anti, pair, y_send, y_recv, p_send, p_recv, z_send, z_recv, local_sem, between):
    zh, y, c = here()
    started = []

    def slot(side, d, core):
        return full.at[member(zh if side == 0 else 1 - zh, y + d, core)["member"]]

    def send(op):
        op.start()
        started.append(op)

    def y_copy(side, kind, source=None):
        d, to, part = KINDS[kind]
        place = halved(slot(side, d, c), part)
        return copy_to(place if source is None else source, place, y_send.at[side, kind], y_recv.at[side, kind], near[to])

    def z_copy(kind, source=None):
        d, to, part = KINDS[kind] if kind >= 0 else (0, 0, 0)
        place = halved(slot(0, d - to, c), part)
        n = max(kind - 3, 0)
        return copy_to(place if source is None else source, place, z_send.at[n], z_recv.at[n], anti)

    def p_copy(side, kind, core, source=None):
        d, to, part = KINDS[kind] if kind >= 0 else (0, 0, 0)
        place = halved(slot(side, d - to, core), part)
        n = side * 9 + kind + 1
        return copy_to(place if source is None else source, place, p_send.at[n], p_recv.at[n], pair)

    def arrivals(side, kinds):
        for kind in kinds:
            if side == 1 and kind >= 4:
                z_copy(kind).wait_recv()
            else:
                y_copy(side, kind).wait_recv()
            if side == 0 and kind in (1, 3):
                send(y_copy(0, kind + 4))
                send(y_copy(0, kind + 3))
            if side == 0 and kind >= 4:
                send(z_copy(kind))
            send(p_copy(side, kind, c))

    send(z_copy(-1, grad))
    for kind in (1, 3, 0, 2):
        send(y_copy(0, kind, grad))
    send(p_copy(0, -1, c, grad))
    mine = pltpu.make_async_copy(grad, slot(0, 0, c), local_sem)
    mine.start()
    between[0]()
    arrivals(0, (1, 3, 0, 2))
    z_copy(-1).wait_recv()
    for kind in (1, 3, 0, 2):
        send(y_copy(1, kind))
    send(p_copy(1, -1, c))
    between[1]()
    arrivals(0, (4, 6, 5, 7))
    arrivals(1, (0, 2, 1, 3, 4, 6, 5, 7))
    mine.wait()
    for op in started:
        op.wait_send()
    for side in range(2):
        for kind in range(-1, 8):
            p_copy(side, kind, 1 - c).wait_recv()


def selectors(owner, pick, place):
    lane, row = lanes(8), lax.broadcasted_iota(jnp.int32, (8, 128), 0)
    for y8 in range(0, NY, 8):
        picked = jnp.zeros((8, 128), F32)
        for i in range(8):
            picked = jnp.where((row == i) & (lane % NY == owner[y8 + i]), 1.0, picked)
        pick[pl.ds(y8, 8), :] = picked
    for d8 in range(0, NY, 8):
        placed = jnp.zeros((8, 128), F32)
        for y in range(NY):
            placed = jnp.where((lane % NY == y) & (row + d8 == owner[y]), 1.0, placed)
        place[pl.ds(d8, 8), :] = placed


def permuted(selector, values):
    rhs = jnp.concatenate(values, axis=1)
    high = rhs.astype(jnp.bfloat16)
    low = (rhs - high.astype(F32)).astype(jnp.bfloat16)
    out = jnp.dot(selector, jnp.concatenate([high, low], axis=0), preferred_element_type=F32)
    return out[:, :128], out[:, 128:]


def weigh(pick, full, pert, k_ref, state, gt):
    def regroup(o, carry):
        for sv in range(SV):
            gt[pl.ds(sv * NZ * NY + o, NZ, stride=NY), :] = full[o, pl.ds(sv * NZ, NZ), :]
        return carry

    lax.fori_loop(0, NY, regroup, 0)
    selector = pick[:, pl.ds(0, 2 * NY)].astype(jnp.bfloat16)

    def reorder(z, carry):
        for sv in range(0, SV, 2):
            places = [pl.ds(pl.multiple_of((sv + i) * NZ * NY + z * NY, NY), NY) for i in range(2)]
            for place, value in zip(places, permuted(selector, [gt[place, :] for place in places])):
                gt[place, :] = value
        return carry

    lax.fori_loop(0, NZ, reorder, 0)

    def body(i, carry):
        z, b = i // 2, lax.rem(i, 2)
        y0 = pl.multiple_of(b * 16, 16)
        grads = [gt[pl.ds(pl.multiple_of(sv * NZ * NY + z * NY + y0, 16), 16), :] for sv in range(SV)]
        k = k_ref[z, pl.ds(y0, 16), :]
        for m in range(M):
            total = None
            for sv in range(SV):
                term = pert[m, sv, z, pl.ds(y0, 16), :].astype(F32) * grads[sv]
                total = term if total is None else total + term
            total = total * k
            for part in range(2):
                start = (y0 + 8 * part) * ROW + z * M + m
                state[pl.ds(start, 8, stride=ROW), :] = total[8 * part : 8 * part + 8]
        return carry

    lax.fori_loop(0, 2 * NZ, body, 0)


def cut_strips(state, vl, vr):
    region = lanes(ROW) // 32

    def body(y, carry):
        turned = [roll(state[pl.ds(pl.multiple_of((8 * h + y) * ROW, ROW), ROW), :], 32 * h) for h in range(4)]
        left, right = turned[0], turned[0]
        for h in range(1, 4):
            left = jnp.where(region == h, turned[h], left)
            right = jnp.where(region == h - 1, turned[h], right)
        rows = pl.ds(pl.multiple_of(y * ROW, ROW), ROW)
        vl[rows, :] = left
        vr[rows, :] = right
        return carry

    lax.fori_loop(0, 8, body, 0)


def evens(row, odd):
    return jnp.concatenate([row[M * (2 * i + odd) : M * (2 * i + odd + 1)] for i in range(4)], axis=0)


def pack_strips(vl, vr, to_left, to_right):
    lane = lanes(ROW // 2) % 32

    def body(y, carry):
        rows = pl.ds(pl.multiple_of(y * ROW, ROW), ROW)
        out = pl.ds(pl.multiple_of(y * ROW // 2, ROW // 2), ROW // 2)
        right, left = vr[rows, :], vl[rows, :]
        to_right[out, :] = jnp.where(lane >= 22, evens(right, 0), roll(evens(right, 1), 118))
        to_left[out, :] = jnp.where(lane < 10, evens(left, 0), roll(evens(left, 1), 10))
        return carry

    lax.fori_loop(0, 8, body, 0)


def unpack_strips(from_left, from_right, vl, vr):
    lane = lanes(ROW) % 32

    def mixed(even, odd):
        return jnp.concatenate([part[M * i : M * i + M] for i in range(4) for part in (even, odd)], axis=0)

    def body(y, carry):
        rows = pl.ds(pl.multiple_of(y * ROW, ROW), ROW)
        packed = pl.ds(pl.multiple_of(y * ROW // 2, ROW // 2), ROW // 2)
        left, right = from_left[packed, :], from_right[packed, :]
        vl[rows, :] = jnp.where(lane >= 22, mixed(left, roll(left, 10)), vl[rows, :])
        vr[rows, :] = jnp.where(lane < 10, mixed(right, roll(right, 118)), vr[rows, :])
        return carry

    lax.fori_loop(0, 8, body, 0)


def merge_strips(state, vl, vr):
    lane = lanes(ROW)
    inner = (lane >= 10) & (lane < 118)

    def body(y, carry):
        rows = pl.ds(pl.multiple_of(y * ROW, ROW), ROW)
        edge = jnp.where(lane % 32 < 10, vl[rows, :], vr[rows, :])
        for h in range(4):
            place = pl.ds(pl.multiple_of((8 * h + y) * ROW, ROW), ROW)
            state[place, :] = jnp.where(inner, state[place, :], roll(edge, -32 * h))
        return carry

    lax.fori_loop(0, 8, body, 0)


def second_pass(pert, k_ref, state, natural, inc, place, norm):
    def body(i, carry):
        z, b = i // 2, lax.rem(i, 2)
        y0 = pl.multiple_of(b * 16, 16)
        factor = norm / k_ref[z, pl.ds(y0, 16), :]
        local = []
        for m in range(M):
            starts = [(y0 + 8 * part) * ROW + z * M + m for part in range(2)]
            local.append(jnp.concatenate([state[pl.ds(s, 8, stride=ROW), :] for s in starts], axis=0))
        for sv in range(SV):
            total = None
            for m in range(M):
                term = pert[m, sv, z, pl.ds(y0, 16), :].astype(F32) * local[m]
                total = term if total is None else total + term
            natural[pl.ds(pl.multiple_of(sv * NZ * NY + z * NY + y0, 16), 16), :] = total * factor
        return carry

    lax.fori_loop(0, 2 * NZ, body, 0)
    selector = place[:, pl.ds(0, 2 * NY)].astype(jnp.bfloat16)

    def reorder(z, carry):
        for sv in range(0, SV, 2):
            values = [natural[pl.ds(pl.multiple_of((sv + i) * NZ * NY + z * NY, NY), NY), :] for i in range(2)]
            for i, value in enumerate(permuted(selector, values)):
                for d8 in range(0, NY, 8):
                    inc[pl.ds(d8 * SV * NZ + (sv + i) * NZ + z, 8, stride=SV * NZ), :] = value[d8 : d8 + 8]
        return carry

    lax.fori_loop(0, NZ, reorder, 0)


def reduce(inc, out, total, other, got, near, anti, pair, p_send, p_recv, send_sem, recv_sem):
    zh, y, c = here()
    started = []

    def block(side, d):
        return (zh if side == 0 else 1 - zh) * RING + lax.rem(y + d + RING, RING)

    def p_copy(n):
        b = block(*ORDER[n])
        return copy_to(inc.at[rows_of(b, 1 - c)], other.at[b], p_send.at[n], p_recv.at[n], pair)

    def send(op):
        op.start()
        started.append(op)

    def rows_of(b, core):
        return pl.ds(pl.multiple_of((2 * b + core) * SV * NZ, SV * NZ), SV * NZ)

    def to(n, side, d, target, part=0):
        return copy_to(
            halved(total.at[block(side, d)], part), halved(got.at[n], part), send_sem.at[n], recv_sem.at[n], target
        )

    def paired(side, *ds):
        for d in ds:
            n = ORDER.index((side, d))
            p_copy(n).wait_recv()
            b = block(side, d)
            total[b] = inc[rows_of(b, c), :] + other[b]

    def add(n, side, d, target, part=0):
        to(n, side, d, target, part).wait_recv()
        b = block(side, d)
        if part == 0:
            total[b] += got[n]
        else:
            half = SV * NZ // 2
            rows = pl.ds(0 if part == 1 else half, half)
            total[b, rows, :] += got[n, rows, :]

    for n in range(len(ORDER)):
        send(p_copy(n))

    for n, d in ((0, 4), (1, 3), (2, -3)):
        paired(1, d)
        send(to(n, 1, d, anti))
    for n, d in ((3, 2), (4, -2), (5, 1), (6, -1)):
        paired(1, d)
        send(to(n, 1, d, near[d]))
    paired(0, 4, 3, -3)
    for n, d in ((7, 1), (8, -1)):
        paired(0, d)
        send(to(n, 0, d, near[d]))
    paired(0, 2, -2)
    paired(1, 0)
    paired(0, 0)
    add(0, 0, 4, anti)
    send(to(9, 0, 4, near[2], 1))
    send(to(10, 0, 4, near[-2], 2))
    add(1, 0, 3, anti)
    send(to(11, 0, 3, near[1]))
    add(2, 0, -3, anti)
    send(to(12, 0, -3, near[-1]))
    for n, d in ((5, 1), (6, -1), (3, 2), (4, -2)):
        add(n, 1, 0, near[d])
    send(to(13, 1, 0, anti))
    add(9, 0, 2, near[2], 1)
    add(11, 0, 2, near[1])
    send(to(14, 0, 2, near[2]))
    add(10, 0, -2, near[-2], 2)
    add(12, 0, -2, near[-1])
    send(to(15, 0, -2, near[-2]))
    for n in (7, 8, 13, 14, 15):
        to(n, 0, 0, anti).wait_recv()
    out[...] = ((total[block(0, 0)] + got[7]) + (got[8] + got[13])) + (got[14] + got[15])
    for op in started:
        op.wait_send()


ORDER = (
    (1, 4), (1, 3), (1, -3), (1, 2), (1, -2), (1, 1), (1, -1), (0, 4), (0, 3), (0, -3), (0, 1), (0, -1),
    (0, 2), (0, -2), (1, 0), (0, 0),
)


def kernel(owner, grad, k_ref, pert_in, out, *scratch, norm, names):
    r = dict(zip(names, scratch))
    zh, y, c = here()
    near = {d: member(zh, y + d, c) for d in (1, 2, -1, -2)}
    anti, pair = member(1 - zh, y, c), member(zh, y, 1 - c)
    pert, s0, s1, l0, l1, r0, r1 = (r[n] for n in ("pert", "s0", "s1", "l0", "l1", "r0", "r1"))
    fetch = pltpu.make_async_copy(pert_in, pert, r["pert_sem"])
    fetch.start()
    greet(list(near.values()) + [anti, pair], tile_links())
    left, right = strip_masks()
    kb, halos = r["kb"], []

    def first():
        k_strips(k_ref, r["kl"], r["kr"])
        halos.append(halo_start(r["kl"], r["kr"], r["hl"], r["hr"], r["h_send"], r["h_recv"]))
        kb[row_at(NY), :] = jnp.zeros((ROW, 128), F32)
        s0[row_at(NY), :] = jnp.zeros((ROW, 128), F32)
        s1[row_at(NY), :] = jnp.zeros((ROW, 128), F32)
        spread(lambda z, b: k_ref[z, pl.ds(8 * b, 8), :], kb, 4)
        coefficients(kb, r["a"], r["q"])

    def second():
        selectors(owner, r["pick"], r["place"])
        halos[0]()
        strip_prepare(r["kl"], r["kr"], r["hl"], r["hr"], r["al"], r["ql"], r["ar"], r["qr"], kb)

    gather(
        grad, r["full"], near, anti, pair, r["y_send"], r["y_recv"], r["p_send"], r["p_recv"], r["z_send"], r["z_recv"],
        r["local_sem"], (first, second),
    )
    fetch.wait()
    weigh(r["pick"], r["full"], pert, k_ref, s0, r["gt"])
    cut_strips(s0, l0, r0)
    pack_strips(l0, r0, r["to_left"], r["to_right"])
    finish = halo_start(r["to_left"], r["to_right"], r["from_left"], r["from_right"], r["s_send"], r["s_recv"])

    def two_main(i, carry):
        main_pass(s0, stepper(s1, r["a"], r["q"]))
        main_pass(s1, stepper(s0, r["a"], r["q"]))
        return carry

    def two_strips(i, carry):
        strip_pass(l0, *left, stepper(l1, r["al"], r["ql"]))
        strip_pass(r0, *right, stepper(r1, r["ar"], r["qr"]))
        strip_pass(l1, *left, stepper(l0, r["al"], r["ql"]))
        strip_pass(r1, *right, stepper(r0, r["ar"], r["qr"]))
        return carry

    lax.fori_loop(0, SWEEPS // 2, two_main, 0)
    finish()
    unpack_strips(r["from_left"], r["from_right"], l0, r0)
    lax.fori_loop(0, SWEEPS // 2, two_strips, 0)
    merge_strips(s0, l0, r0)
    second_pass(pert, k_ref, s0, r["gt"], r["inc"], r["place"], norm)
    reduce(
        r["inc"], out, r["total"], r["other"], r["got"], near, anti, pair,
        r["rp_send"], r["rp_recv"], r["r_send"], r["r_recv"],
    )


def body(perturbations, gradient_store, diffusivity, slab_owner):
    members = perturbations.shape[0] * lax.axis_size("member")
    pert = perturbations.reshape(M, SV, NZ, NY, 128)
    grad = gradient_store.reshape(SV * NZ, 128)
    dma = pltpu.SemaphoreType.DMA

    def f32(*shape):
        return pltpu.VMEM(shape + (128,), F32)

    scratch = {
        "pert": pltpu.VMEM(pert.shape, pert.dtype), "pert_sem": dma,
        "full": f32(4 * RING, SV * NZ), "gt": f32(SV * NZ * NY), "pick": f32(NY), "place": f32(NY),
        "s0": f32((NY + 1) * ROW), "s1": f32((NY + 1) * ROW), "kb": f32((NY + 1) * ROW),
        "a": f32(NY * ROW), "q": f32(NY * ROW),
        **{n: f32(9 * ROW) for n in ("l0", "l1", "r0", "r1")},
        **{n: f32(8 * ROW) for n in ("al", "ql", "ar", "qr")},
        **{n: f32(NZ, 8) for n in ("kl", "kr", "hl", "hr")},
        **{n: f32(4 * ROW) for n in ("to_left", "to_right", "from_left", "from_right")},
        "inc": f32(NY * SV * NZ),
        **{n: f32(2 * RING, SV * NZ) for n in ("total", "other", "got")},
        **{n: dma((2, 8)) for n in ("y_send", "y_recv")},
        **{n: dma((18,)) for n in ("p_send", "p_recv")},
        **{n: dma((5,)) for n in ("z_send", "z_recv")},
        "local_sem": dma,
        **{n: dma((2,)) for n in ("h_send", "h_recv", "s_send", "s_recv")},
        **{n: dma((16,)) for n in ("rp_send", "rp_recv", "r_send", "r_recv")},
    }
    out = pl.pallas_call(
        functools.partial(kernel, norm=1.0 / (members - 1), names=tuple(scratch)),
        out_shape=jax.ShapeDtypeStruct((SV * NZ, 128), F32),
        in_specs=[SMEM, VMEM, VMEM, pl.BlockSpec(memory_space=pl.ANY)],
        out_specs=VMEM,
        scratch_shapes=list(scratch.values()),
        compiler_params=pltpu.CompilerParams(vmem_limit_bytes=LIMIT, collective_id=0, has_side_effects=True),
    )(slab_owner, grad, diffusivity, pert)
    return out.reshape(gradient_store.shape)


def solution(mesh):
    in_specs = (
        P("member", None, None, None, None, "tile"),
        P(None, None, None, "member", "tile"),
        P(None, None, "tile"),
        P(),
    )
    out_specs = P(None, None, None, "member", "tile")
    return jax.shard_map(body, mesh=mesh, in_specs=in_specs, out_specs=out_specs, check_vma=False)
```

```python
import functools

import jax
import jax.numpy as jnp
from jax import lax
from jax.experimental import pallas as pl
from jax.experimental.pallas import tpu as pltpu
from jax.sharding import PartitionSpec as P

MESH = pl.DeviceIdType.MESH
F32 = jnp.float32
SWEEPS = 10
SV = 10
M = 8
NZ = 8
NY = 32
RING = 8
ROW = NZ * M
VMEM = pl.BlockSpec(memory_space=pltpu.VMEM)
SMEM = pl.BlockSpec(memory_space=pltpu.SMEM)
LIMIT = 60 * 1024 * 1024
UNROLL = 2


def lanes(rows):
    return lax.broadcasted_iota(jnp.int32, (rows, 128), 1)


def roll(value, shift):
    shift = shift % 128
    return value if shift == 0 else pltpu.roll(value, shift, 1)


def up(row, above):
    cut = row.shape[0] - M
    return jnp.concatenate([row[:cut] + above[M:], row[cut:]], axis=0)


def sideways(row):
    return roll(row, 1) + roll(row, 127)


def row_at(y):
    return pl.ds(y * ROW if isinstance(y, int) else pl.multiple_of(y * ROW, ROW), ROW)


def rows_pass(src, count, first, p0, pu, beside, emit, unroll):
    def body(y, carry):
        p0, pu, cur = carry
        nxt = src[row_at(y + 1), :]
        u = up(nxt, cur)
        four = u + jnp.concatenate([p0, pu[: ROW - M]], axis=0)
        emit(row_at(y), cur, four + beside(row_at(y), cur))
        return cur[:M], u, nxt

    lax.fori_loop(0, count, body, (p0, pu, first), unroll=unroll)


def rotated(rows, cur):
    return sideways(cur)


def main_pass(src, beside, emit, unroll=UNROLL):
    first = src[row_at(0), :]
    rows_pass(src, NY, first, jnp.zeros((M, 128), F32), first, beside, emit, unroll)


def strip_pass(src, lo, hi, beside, emit, unroll=UNROLL):
    first, last = src[row_at(0), :], src[row_at(7), :]
    prev = jnp.where(lo, 0.0, roll(last, 32))
    src[row_at(8), :] = jnp.where(hi, 0.0, roll(first, 96))
    rows_pass(src, 8, first, prev[:M], up(first, prev), beside, emit, unroll)


def strip_masks():
    lane = lanes(ROW)
    left = ((lane >= 118) | (lane < 22), (lane >= 86) & (lane < 118))
    right = ((lane >= 106) | (lane < 10), (lane >= 74) & (lane < 106))
    return left, right


def coefficients(src, dst_a, dst_q, strip=None):
    def emit(rows, cur, total):
        dst_a[rows, :] = 1.0 - cur * total
        dst_q[rows, :] = cur * cur

    if strip is None:
        main_pass(src, rotated, emit, 4)
    else:
        strip_pass(src, *strip, rotated, emit, 4)


def parts(value):
    high = value.astype(jnp.bfloat16)
    return high, (value - high.astype(F32)).astype(jnp.bfloat16)


def pair_sums(value, ring):
    return jnp.dot(jnp.concatenate(parts(value), axis=1), ring[...], preferred_element_type=F32)


def ring_matrix(ring):
    row, col = (lax.broadcasted_iota(jnp.int32, (256, 128), i) for i in range(2))
    apart = (row - col + 128) % 128
    ring[...] = jnp.where((apart == 1) | (apart == 127), 1.0, 0.0).astype(jnp.bfloat16)


def advance(field, pairs, new_field, a, q, start, count, carry, keep):
    p0, pu, cur = carry
    for i in range(count):
        y = start + i
        nxt = field[row_at(y + 1), :]
        u = up(nxt, cur)
        total = (u + jnp.concatenate([p0, pu[: ROW - M]], axis=0)) + pairs[row_at(y), :]
        new = a[row_at(y), :] * cur + q[row_at(y), :] * total
        new_field[row_at(y), :] = new
        keep(i, new)
        p0, pu, cur = cur[:M], u, nxt
    return p0, pu, cur


CHUNK = 4
CHUNKS = 8


def main_sweep(src, dst, a, q, ring):
    (field, pairs), (new_field, new_pairs) = src, dst

    def body(i, carry):
        for n in range(CHUNKS):
            y, news = (i * CHUNKS + n) * CHUNK, []
            carry = advance(field, pairs, new_field, a, q, y, CHUNK, carry, lambda i, new: news.append(new))
            rows = pl.ds(pl.multiple_of(y * ROW, CHUNK * ROW), CHUNK * ROW)
            value = jnp.concatenate(news, axis=0)
            new_pairs[rows, :] = sideways(value) if n % 3 == 1 else pair_sums(value, ring)
        return carry

    first = field[row_at(0), :]
    lax.fori_loop(0, NY // (CHUNKS * CHUNK), body, (jnp.zeros((M, 128), F32), first, first))


def strip_sweeps(sides, ring):
    starts = []
    for (field, pairs), dst, a, q, (lo, hi) in sides:
        first, last = field[row_at(0), :], field[row_at(7), :]
        prev = jnp.where(lo, 0.0, roll(last, 32))
        field[row_at(8), :] = jnp.where(hi, 0.0, roll(first, 96))
        starts.append((prev[:M], up(first, prev), first))
    for half in range(8 // CHUNK):
        for n, ((field, pairs), (new_field, new_pairs), a, q, masks) in enumerate(sides):
            news = []
            starts[n] = advance(
                field, pairs, new_field, a, q, half * CHUNK, CHUNK, starts[n], lambda i, new: news.append(new)
            )
            new_pairs[pl.ds(half * CHUNK * ROW, CHUNK * ROW), :] = pair_sums(jnp.concatenate(news, axis=0), ring)


def k_strips(k_ref, left_ref, right_ref):
    region = lanes(8) // 32
    for z in range(NZ):
        turned = [roll(k_ref[z, pl.ds(8 * h, 8), :], 32 * h) for h in range(4)]
        left, right = turned[0], turned[0]
        for h in range(1, 4):
            left = jnp.where(region == h, turned[h], left)
            right = jnp.where(region == h - 1, turned[h], right)
        left_ref[z] = left
        right_ref[z] = right


def spread(value_of, dst, blocks, pad=True):
    def body(z, carry):
        for b in range(blocks):
            value = value_of(z, b)
            for m in range(M):
                dst[pl.ds(b * 8 * ROW + z * M + m, 8, stride=ROW), :] = value
        return carry

    lax.fori_loop(0, NZ, body, 0)


def strip_prepare(kl_ref, kr_ref, hl_ref, hr_ref, al, ql, ar, qr, kb):
    lane = lanes(8) % 32
    left, right = strip_masks()
    spread(lambda z, b: jnp.where(lane >= 22, hl_ref[z], kl_ref[z]), kb, 1)
    coefficients(kb, al, ql, left)
    spread(lambda z, b: jnp.where(lane < 10, hr_ref[z], kr_ref[z]), kb, 1)
    coefficients(kb, ar, qr, right)


def member(zh, y, c):
    return {"member": (zh * RING + lax.rem(y + RING, RING)) * 2 + c}


def here():
    i = lax.axis_index("member")
    return i // (2 * RING), lax.rem(i // 2, RING), lax.rem(i, 2)


def greet(targets, conditional=()):
    barrier = pltpu.get_barrier_semaphore()
    count = len(targets)
    for target in targets:
        pl.semaphore_signal(barrier, inc=1, device_id=target, device_id_type=MESH)
    for condition, target in conditional:
        @pl.when(condition)
        def _():
            pl.semaphore_signal(barrier, inc=1, device_id=target, device_id_type=MESH)

        count = count + jnp.where(condition, 1, 0)
    pl.semaphore_wait(barrier, count)


def copy_to(src, dst, send, recv, target):
    return pltpu.make_async_remote_copy(
        src_ref=src, dst_ref=dst, send_sem=send, recv_sem=recv, device_id=target, device_id_type=MESH
    )


def tile_links():
    t, n = lax.axis_index("tile"), lax.axis_size("tile")
    return (t > 0, {"tile": lax.rem(t + n - 1, n)}), (t < n - 1, {"tile": lax.rem(t + 1, n)})


def halo_start(to_left, to_right, from_left, from_right, send, recv):
    (has_left, left), (has_right, right) = tile_links()
    rightward = copy_to(to_right, from_left, send.at[0], recv.at[0], right)
    leftward = copy_to(to_left, from_right, send.at[1], recv.at[1], left)

    @pl.when(has_right)
    def _():
        rightward.start()

    @pl.when(has_left)
    def _():
        leftward.start()

    @pl.when(jnp.logical_not(has_left))
    def _():
        from_left[...] = jnp.zeros(from_left.shape, F32)

    @pl.when(jnp.logical_not(has_right))
    def _():
        from_right[...] = jnp.zeros(from_right.shape, F32)

    def finish():
        @pl.when(has_right)
        def _():
            rightward.wait_send()
            leftward.wait_recv()

        @pl.when(has_left)
        def _():
            leftward.wait_send()
            rightward.wait_recv()

    return finish


KINDS = {
    0: (0, 1, 0), 1: (0, 2, 0), 2: (0, -1, 0), 3: (0, -2, 0),
    4: (-2, 1, 0), 5: (-2, 2, 1), 6: (2, -1, 0), 7: (2, -2, 2),
}


def halved(ref, part):
    half = SV * NZ // 2
    return ref if part == 0 else ref.at[pl.ds(0 if part == 1 else half, half)]


def gather(grad, full, near, anti, pair, y_send, y_recv, p_send, p_recv, z_send, z_recv, local_sem, gt, between):
    zh, y, c = here()
    started = []

    def slot(side, d, core):
        return full.at[member(zh if side == 0 else 1 - zh, y + d, core)["member"]]

    def send(op):
        op.start()
        started.append(op)

    def y_copy(side, kind, source=None):
        d, to, part = KINDS[kind]
        place = halved(slot(side, d, c), part)
        return copy_to(place if source is None else source, place, y_send.at[side, kind], y_recv.at[side, kind], near[to])

    def z_copy(kind, source=None):
        d, to, part = KINDS[kind] if kind >= 0 else (0, 0, 0)
        place = halved(slot(0, d - to, c), part)
        n = max(kind - 3, 0)
        return copy_to(place if source is None else source, place, z_send.at[n], z_recv.at[n], anti)

    def p_copy(side, kind, core, source=None):
        d, to, part = KINDS[kind] if kind >= 0 else (0, 0, 0)
        place = halved(slot(side, d - to, core), part)
        n = side * 9 + kind + 1
        return copy_to(place if source is None else source, place, p_send.at[n], p_recv.at[n], pair)

    def arrivals(side, kinds):
        for kind in kinds:
            if side == 1 and kind >= 4:
                z_copy(kind).wait_recv()
            else:
                y_copy(side, kind).wait_recv()
            if side == 0 and kind in (1, 3):
                send(y_copy(0, kind + 4))
                send(y_copy(0, kind + 3))
            if side == 0 and kind >= 4:
                send(z_copy(kind))
            send(p_copy(side, kind, c))

    send(z_copy(-1, grad))
    for kind in (1, 3, 0, 2):
        send(y_copy(0, kind, grad))
    send(p_copy(0, -1, c, grad))
    mine = pltpu.make_async_copy(grad, slot(0, 0, c), local_sem)
    mine.start()
    between[0]()
    arrivals(0, (1, 3, 0, 2))
    z_copy(-1).wait_recv()
    for kind in (1, 3, 0, 2):
        send(y_copy(1, kind))
    send(p_copy(1, -1, c))
    between[1]()

    def unload(side, core, *ds):
        for d in ds:
            o = member(zh if side == 0 else 1 - zh, y + d, core)["member"]
            for sv in range(SV):
                gt[pl.ds(sv * NZ * NY + o, NZ, stride=NY), :] = full[o, pl.ds(sv * NZ, NZ), :]

    def from_pair(side, *kinds):
        for kind in kinds:
            p_copy(side, kind, 1 - c).wait_recv()

    mine.wait()
    unload(0, c, 0, 1, -1, 2, -2)
    unload(1, c, 0)
    arrivals(0, (4, 6, 5, 7))
    unload(0, c, 3, -3, 4)
    arrivals(1, (0, 2, 1, 3))
    unload(1, c, 1, -1, 2, -2)
    from_pair(0, -1, 0, 1, 2, 3)
    unload(0, 1 - c, 0, 1, -1, 2, -2)
    arrivals(1, (4, 6, 5, 7))
    unload(1, c, 3, -3, 4)
    from_pair(0, 4, 5, 6, 7)
    unload(0, 1 - c, 3, -3, 4)
    from_pair(1, -1, 0, 1, 2, 3)
    unload(1, 1 - c, 0, 1, -1, 2, -2)
    from_pair(1, 4, 5, 6, 7)
    unload(1, 1 - c, 3, -3, 4)
    for op in started:
        op.wait_send()


def selectors(owner, pick, place):
    lane, row = lanes(8), lax.broadcasted_iota(jnp.int32, (8, 128), 0)
    for y8 in range(0, NY, 8):
        picked = jnp.zeros((8, 128), F32)
        for i in range(8):
            picked = jnp.where((row == i) & (lane % NY == owner[y8 + i]), 1.0, picked)
        pick[pl.ds(y8, 8), :] = picked
    for d8 in range(0, NY, 8):
        placed = jnp.zeros((8, 128), F32)
        for y in range(NY):
            placed = jnp.where((lane % NY == y) & (row + d8 == owner[y]), 1.0, placed)
        place[pl.ds(d8, 8), :] = placed


def permuted(selector, values):
    rhs = jnp.concatenate(values, axis=1)
    high = rhs.astype(jnp.bfloat16)
    low = (rhs - high.astype(F32)).astype(jnp.bfloat16)
    out = jnp.dot(selector, jnp.concatenate([high, low], axis=0), preferred_element_type=F32)
    return out[:, :128], out[:, 128:]


def weigh(pick, pert, k_ref, state, gt):
    selector = pick[:, pl.ds(0, 2 * NY)].astype(jnp.bfloat16)

    def reorder(z, carry):
        for sv in range(0, SV, 2):
            places = [pl.ds(pl.multiple_of((sv + i) * NZ * NY + z * NY, NY), NY) for i in range(2)]
            for place, value in zip(places, permuted(selector, [gt[place, :] for place in places])):
                gt[place, :] = value
        return carry

    lax.fori_loop(0, NZ, reorder, 0)

    def body(i, carry):
        z, b = i // 2, lax.rem(i, 2)
        y0 = pl.multiple_of(b * 16, 16)
        grads = [gt[pl.ds(pl.multiple_of(sv * NZ * NY + z * NY + y0, 16), 16), :] for sv in range(SV)]
        k = k_ref[z, pl.ds(y0, 16), :]
        for m in range(M):
            total = None
            for sv in range(SV):
                term = pert[m, sv, z, pl.ds(y0, 16), :].astype(F32) * grads[sv]
                total = term if total is None else total + term
            total = total * k
            for part in range(2):
                start = (y0 + 8 * part) * ROW + z * M + m
                state[pl.ds(start, 8, stride=ROW), :] = total[8 * part : 8 * part + 8]
        return carry

    lax.fori_loop(0, 2 * NZ, body, 0)


def cut_strips(state, pairs, vl, vr, ring):
    region = lanes(ROW) // 32

    def body(y, carry):
        quarters = [state[row_at(8 * h + y), :] for h in range(4)]
        turned = [roll(row, 32 * h) for h, row in enumerate(quarters)]
        sums = pair_sums(jnp.concatenate(quarters, axis=0), ring)
        for h in range(4):
            pairs[row_at(8 * h + y), :] = sums[h * ROW : (h + 1) * ROW]
        left, right = turned[0], turned[0]
        for h in range(1, 4):
            left = jnp.where(region == h, turned[h], left)
            right = jnp.where(region == h - 1, turned[h], right)
        rows = pl.ds(pl.multiple_of(y * ROW, ROW), ROW)
        vl[rows, :] = left
        vr[rows, :] = right
        return carry

    lax.fori_loop(0, 8, body, 0)


def evens(row, odd):
    return jnp.concatenate([row[M * (2 * i + odd) : M * (2 * i + odd + 1)] for i in range(4)], axis=0)


def pack_strips(vl, vr, to_left, to_right):
    lane = lanes(ROW // 2) % 32

    def body(y, carry):
        rows = pl.ds(pl.multiple_of(y * ROW, ROW), ROW)
        out = pl.ds(pl.multiple_of(y * ROW // 2, ROW // 2), ROW // 2)
        right, left = vr[rows, :], vl[rows, :]
        to_right[out, :] = jnp.where(lane >= 22, evens(right, 0), roll(evens(right, 1), 118))
        to_left[out, :] = jnp.where(lane < 10, evens(left, 0), roll(evens(left, 1), 10))
        return carry

    lax.fori_loop(0, 8, body, 0)


def unpack_strips(from_left, from_right, vl, vr, lp, rp, ring):
    lane = lanes(ROW) % 32

    def mixed(even, odd):
        return jnp.concatenate([part[M * i : M * i + M] for i in range(4) for part in (even, odd)], axis=0)

    def body(y, carry):
        rows = pl.ds(pl.multiple_of(y * ROW, ROW), ROW)
        packed = pl.ds(pl.multiple_of(y * ROW // 2, ROW // 2), ROW // 2)
        left, right = from_left[packed, :], from_right[packed, :]
        left = jnp.where(lane >= 22, mixed(left, roll(left, 10)), vl[rows, :])
        right = jnp.where(lane < 10, mixed(right, roll(right, 118)), vr[rows, :])
        vl[rows, :] = left
        vr[rows, :] = right
        sums = pair_sums(jnp.concatenate([left, right], axis=0), ring)
        lp[rows, :] = sums[:ROW]
        rp[rows, :] = sums[ROW:]
        return carry

    lax.fori_loop(0, 8, body, 0)


def merge_strips(state, vl, vr):
    lane = lanes(ROW)
    inner = (lane >= 10) & (lane < 118)

    def body(y, carry):
        rows = pl.ds(pl.multiple_of(y * ROW, ROW), ROW)
        edge = jnp.where(lane % 32 < 10, vl[rows, :], vr[rows, :])
        for h in range(4):
            place = pl.ds(pl.multiple_of((8 * h + y) * ROW, ROW), ROW)
            state[place, :] = jnp.where(inner, state[place, :], roll(edge, -32 * h))
        return carry

    lax.fori_loop(0, 8, body, 0)


def second_pass(pert, k_ref, state, natural, inc, place, norm):
    def body(i, carry):
        z, b = i // 2, lax.rem(i, 2)
        y0 = pl.multiple_of(b * 16, 16)
        factor = norm / k_ref[z, pl.ds(y0, 16), :]
        local = []
        for m in range(M):
            starts = [(y0 + 8 * part) * ROW + z * M + m for part in range(2)]
            local.append(jnp.concatenate([state[pl.ds(s, 8, stride=ROW), :] for s in starts], axis=0))
        for sv in range(SV):
            total = None
            for m in range(M):
                term = pert[m, sv, z, pl.ds(y0, 16), :].astype(F32) * local[m]
                total = term if total is None else total + term
            natural[pl.ds(pl.multiple_of(sv * NZ * NY + z * NY + y0, 16), 16), :] = total * factor
        return carry

    lax.fori_loop(0, 2 * NZ, body, 0)
    selector = place[:, pl.ds(0, 2 * NY)].astype(jnp.bfloat16)

    def reorder(z, carry):
        for sv in range(0, SV, 2):
            values = [natural[pl.ds(pl.multiple_of((sv + i) * NZ * NY + z * NY, NY), NY), :] for i in range(2)]
            for i, value in enumerate(permuted(selector, values)):
                for d8 in range(0, NY, 8):
                    inc[pl.ds(d8 * SV * NZ + (sv + i) * NZ + z, 8, stride=SV * NZ), :] = value[d8 : d8 + 8]
        return carry

    lax.fori_loop(0, NZ, reorder, 0)


def reduce(inc, out, total, other, got, near, anti, pair, p_send, p_recv, send_sem, recv_sem):
    zh, y, c = here()
    started = []

    def block(side, d):
        return (zh if side == 0 else 1 - zh) * RING + lax.rem(y + d + RING, RING)

    def p_copy(n):
        b = block(*ORDER[n])
        return copy_to(inc.at[rows_of(b, 1 - c)], other.at[b], p_send.at[n], p_recv.at[n], pair)

    def send(op):
        op.start()
        started.append(op)

    def rows_of(b, core):
        return pl.ds(pl.multiple_of((2 * b + core) * SV * NZ, SV * NZ), SV * NZ)

    def to(n, side, d, target, part=0):
        return copy_to(
            halved(total.at[block(side, d)], part), halved(got.at[n], part), send_sem.at[n], recv_sem.at[n], target
        )

    def paired(side, *ds):
        for d in ds:
            n = ORDER.index((side, d))
            p_copy(n).wait_recv()
            b = block(side, d)
            total[b] = inc[rows_of(b, c), :] + other[b]

    def add(n, side, d, target, part=0):
        to(n, side, d, target, part).wait_recv()
        b = block(side, d)
        if part == 0:
            total[b] += got[n]
        else:
            half = SV * NZ // 2
            rows = pl.ds(0 if part == 1 else half, half)
            total[b, rows, :] += got[n, rows, :]

    for n in range(len(ORDER)):
        send(p_copy(n))

    for n, d in ((0, 4), (1, 3), (2, -3)):
        paired(1, d)
        send(to(n, 1, d, anti))
    for n, d in ((3, 2), (4, -2), (5, 1), (6, -1)):
        paired(1, d)
        send(to(n, 1, d, near[d]))
    paired(0, 4, 3, -3)
    for n, d in ((7, 1), (8, -1)):
        paired(0, d)
        send(to(n, 0, d, near[d]))
    paired(0, 2, -2)
    paired(1, 0)
    paired(0, 0)
    add(0, 0, 4, anti)
    send(to(9, 0, 4, near[2], 1))
    send(to(10, 0, 4, near[-2], 2))
    add(1, 0, 3, anti)
    send(to(11, 0, 3, near[1]))
    add(2, 0, -3, anti)
    send(to(12, 0, -3, near[-1]))
    for n, d in ((5, 1), (6, -1), (3, 2), (4, -2)):
        add(n, 1, 0, near[d])
    send(to(13, 1, 0, anti))
    add(9, 0, 2, near[2], 1)
    add(11, 0, 2, near[1])
    send(to(14, 0, 2, near[2]))
    add(10, 0, -2, near[-2], 2)
    add(12, 0, -2, near[-1])
    send(to(15, 0, -2, near[-2]))
    for n in (7, 8, 13, 14, 15):
        to(n, 0, 0, anti).wait_recv()
    out[...] = ((total[block(0, 0)] + got[7]) + (got[8] + got[13])) + (got[14] + got[15])
    for op in started:
        op.wait_send()


ORDER = (
    (1, 4), (1, 3), (1, -3), (1, 2), (1, -2), (1, 1), (1, -1), (0, 4), (0, 3), (0, -3), (0, 1), (0, -1),
    (0, 2), (0, -2), (1, 0), (0, 0),
)


def kernel(owner, grad, k_ref, pert_in, out, *scratch, norm, names):
    r = dict(zip(names, scratch))
    zh, y, c = here()
    near = {d: member(zh, y + d, c) for d in (1, 2, -1, -2)}
    anti, pair = member(1 - zh, y, c), member(zh, y, 1 - c)
    pert, s0, s1, l0, l1, r0, r1 = (r[n] for n in ("pert", "s0", "s1", "l0", "l1", "r0", "r1"))
    fetch = pltpu.make_async_copy(pert_in, pert, r["pert_sem"])
    fetch.start()
    greet(list(near.values()) + [anti, pair], tile_links())
    left, right = strip_masks()
    kb, halos = r["kb"], []

    def first():
        ring_matrix(r["ring"])
        k_strips(k_ref, r["kl"], r["kr"])
        halos.append(halo_start(r["kl"], r["kr"], r["hl"], r["hr"], r["h_send"], r["h_recv"]))
        kb[row_at(NY), :] = jnp.zeros((ROW, 128), F32)
        s0[row_at(NY), :] = jnp.zeros((ROW, 128), F32)
        s1[row_at(NY), :] = jnp.zeros((ROW, 128), F32)
        spread(lambda z, b: k_ref[z, pl.ds(8 * b, 8), :], kb, 4)
        coefficients(kb, r["a"], r["q"])

    def second():
        selectors(owner, r["pick"], r["place"])
        halos[0]()
        strip_prepare(r["kl"], r["kr"], r["hl"], r["hr"], r["al"], r["ql"], r["ar"], r["qr"], kb)

    gather(
        grad, r["full"], near, anti, pair, r["y_send"], r["y_recv"], r["p_send"], r["p_recv"], r["z_send"], r["z_recv"],
        r["local_sem"], r["gt"], (first, second),
    )
    fetch.wait()
    weigh(r["pick"], pert, k_ref, s0, r["gt"])
    cut_strips(s0, r["sp0"], l0, r0, r["ring"])
    pack_strips(l0, r0, r["to_left"], r["to_right"])
    finish = halo_start(r["to_left"], r["to_right"], r["from_left"], r["from_right"], r["s_send"], r["s_recv"])

    main = ((s0, r["sp0"]), (s1, r["sp1"]))
    lefts = ((l0, r["lp0"]), (l1, r["lp1"]))
    rights = ((r0, r["rp0"]), (r1, r["rp1"]))

    def two_main(i, carry):
        for n in range(2):
            main_sweep(main[n], main[1 - n], r["a"], r["q"], r["ring"])
        return carry

    def two_strips(i, carry):
        for n in range(2):
            strip_sweeps(
                ((lefts[n], lefts[1 - n], r["al"], r["ql"], left), (rights[n], rights[1 - n], r["ar"], r["qr"], right)),
                r["ring"],
            )
        return carry

    lax.fori_loop(0, SWEEPS // 2, two_main, 0)
    finish()
    unpack_strips(r["from_left"], r["from_right"], l0, r0, r["lp0"], r["rp0"], r["ring"])
    lax.fori_loop(0, SWEEPS // 2, two_strips, 0)
    merge_strips(s0, l0, r0)
    second_pass(pert, k_ref, s0, r["gt"], r["inc"], r["place"], norm)
    reduce(
        r["inc"], out, r["total"], r["other"], r["got"], near, anti, pair,
        r["rp_send"], r["rp_recv"], r["r_send"], r["r_recv"],
    )


def body(perturbations, gradient_store, diffusivity, slab_owner):
    members = perturbations.shape[0] * lax.axis_size("member")
    pert = perturbations.reshape(M, SV, NZ, NY, 128)
    grad = gradient_store.reshape(SV * NZ, 128)
    dma = pltpu.SemaphoreType.DMA

    def f32(*shape):
        return pltpu.VMEM(shape + (128,), F32)

    scratch = {
        "pert": pltpu.VMEM(pert.shape, pert.dtype), "pert_sem": dma,
        "full": f32(4 * RING, SV * NZ), "gt": f32(SV * NZ * NY), "pick": f32(NY), "place": f32(NY),
        "s0": f32((NY + 1) * ROW), "s1": f32((NY + 1) * ROW), "kb": f32((NY + 1) * ROW),
        **{n: f32(NY * ROW) for n in ("a", "q", "sp0", "sp1")},
        "ring": pltpu.VMEM((256, 128), jnp.bfloat16),
        **{n: f32(9 * ROW) for n in ("l0", "l1", "r0", "r1")},
        **{n: f32(8 * ROW) for n in ("al", "ql", "ar", "qr", "lp0", "lp1", "rp0", "rp1")},
        **{n: f32(NZ, 8) for n in ("kl", "kr", "hl", "hr")},
        **{n: f32(4 * ROW) for n in ("to_left", "to_right", "from_left", "from_right")},
        "inc": f32(NY * SV * NZ),
        **{n: f32(2 * RING, SV * NZ) for n in ("total", "other", "got")},
        **{n: dma((2, 8)) for n in ("y_send", "y_recv")},
        **{n: dma((18,)) for n in ("p_send", "p_recv")},
        **{n: dma((5,)) for n in ("z_send", "z_recv")},
        "local_sem": dma,
        **{n: dma((2,)) for n in ("h_send", "h_recv", "s_send", "s_recv")},
        **{n: dma((16,)) for n in ("rp_send", "rp_recv", "r_send", "r_recv")},
    }
    out = pl.pallas_call(
        functools.partial(kernel, norm=1.0 / (members - 1), names=tuple(scratch)),
        out_shape=jax.ShapeDtypeStruct((SV * NZ, 128), F32),
        in_specs=[SMEM, VMEM, VMEM, pl.BlockSpec(memory_space=pl.ANY)],
        out_specs=VMEM,
        scratch_shapes=list(scratch.values()),
        compiler_params=pltpu.CompilerParams(vmem_limit_bytes=LIMIT, collective_id=0, has_side_effects=True),
    )(slab_owner, grad, diffusivity, pert)
    return out.reshape(gradient_store.shape)


def solution(mesh):
    in_specs = (
        P("member", None, None, None, None, "tile"),
        P(None, None, None, "member", "tile"),
        P(None, None, "tile"),
        P(),
    )
    out_specs = P(None, None, None, "member", "tile")
    return jax.shard_map(body, mesh=mesh, in_specs=in_specs, out_specs=out_specs, check_vma=False)
```

```python
import functools

import jax
import jax.numpy as jnp
from jax import lax
from jax.experimental import pallas as pl
from jax.experimental.pallas import tpu as pltpu
from jax.sharding import PartitionSpec as P

MESH = pl.DeviceIdType.MESH
F32 = jnp.float32
SWEEPS = 10
SV = 10
M = 8
NZ = 8
NY = 32
RING = 8
ROW = NZ * M
VMEM = pl.BlockSpec(memory_space=pltpu.VMEM)
SMEM = pl.BlockSpec(memory_space=pltpu.SMEM)
LIMIT = 60 * 1024 * 1024
UNROLL = 2


def lanes(rows):
    return lax.broadcasted_iota(jnp.int32, (rows, 128), 1)


def roll(value, shift):
    shift = shift % 128
    return value if shift == 0 else pltpu.roll(value, shift, 1)


def up(row, above):
    cut = row.shape[0] - M
    return jnp.concatenate([row[:cut] + above[M:], row[cut:]], axis=0)


def sideways(row):
    return roll(row, 1) + roll(row, 127)


def row_at(y):
    return pl.ds(y * ROW if isinstance(y, int) else pl.multiple_of(y * ROW, ROW), ROW)


def rows_pass(src, count, first, p0, pu, beside, emit, unroll):
    def body(y, carry):
        p0, pu, cur = carry
        nxt = src[row_at(y + 1), :]
        u = up(nxt, cur)
        four = u + jnp.concatenate([p0, pu[: ROW - M]], axis=0)
        emit(row_at(y), cur, four + beside(row_at(y), cur))
        return cur[:M], u, nxt

    lax.fori_loop(0, count, body, (p0, pu, first), unroll=unroll)


def rotated(rows, cur):
    return sideways(cur)


def main_pass(src, beside, emit, unroll=UNROLL):
    first = src[row_at(0), :]
    rows_pass(src, NY, first, jnp.zeros((M, 128), F32), first, beside, emit, unroll)


def strip_pass(src, lo, hi, beside, emit, unroll=UNROLL):
    first, last = src[row_at(0), :], src[row_at(7), :]
    prev = jnp.where(lo, 0.0, roll(last, 32))
    src[row_at(8), :] = jnp.where(hi, 0.0, roll(first, 96))
    rows_pass(src, 8, first, prev[:M], up(first, prev), beside, emit, unroll)


def strip_masks():
    lane = lanes(ROW)
    left = ((lane >= 118) | (lane < 22), (lane >= 86) & (lane < 118))
    right = ((lane >= 106) | (lane < 10), (lane >= 74) & (lane < 106))
    return left, right


def coefficients(src, dst_a, dst_q, strip=None):
    def emit(rows, cur, total):
        dst_a[rows, :] = 1.0 - cur * total
        dst_q[rows, :] = cur * cur

    if strip is None:
        main_pass(src, rotated, emit, 4)
    else:
        strip_pass(src, *strip, rotated, emit, 4)


def parts(value):
    high = value.astype(jnp.bfloat16)
    return high, (value - high.astype(F32)).astype(jnp.bfloat16)


def pair_sums(value, ring):
    return jnp.dot(jnp.concatenate(parts(value), axis=1), ring[...], preferred_element_type=F32)


def ring_matrix(ring):
    row, col = (lax.broadcasted_iota(jnp.int32, (256, 128), i) for i in range(2))
    apart = (row - col + 128) % 128
    ring[...] = jnp.where((apart == 1) | (apart == 127), 1.0, 0.0).astype(jnp.bfloat16)


def advance(field, pairs, new_field, a, q, start, count, carry, keep):
    p0, pu, cur = carry
    for i in range(count):
        y = start + i
        nxt = field[row_at(y + 1), :]
        u = up(nxt, cur)
        total = (u + jnp.concatenate([p0, pu[: ROW - M]], axis=0)) + pairs[row_at(y), :]
        new = a[row_at(y), :] * cur + q[row_at(y), :] * total
        new_field[row_at(y), :] = new
        keep(i, new)
        p0, pu, cur = cur[:M], u, nxt
    return p0, pu, cur


CHUNK = 4
CHUNKS = 8


def main_sweep(src, dst, a, q, ring):
    (field, pairs), (new_field, new_pairs) = src, dst

    def body(i, carry):
        for n in range(CHUNKS):
            y, news = (i * CHUNKS + n) * CHUNK, []
            carry = advance(field, pairs, new_field, a, q, y, CHUNK, carry, lambda i, new: news.append(new))
            rows = pl.ds(pl.multiple_of(y * ROW, CHUNK * ROW), CHUNK * ROW)
            value = jnp.concatenate(news, axis=0)
            new_pairs[rows, :] = sideways(value) if n % 3 == 1 else pair_sums(value, ring)
        return carry

    first = field[row_at(0), :]
    lax.fori_loop(0, NY // (CHUNKS * CHUNK), body, (jnp.zeros((M, 128), F32), first, first))


def strip_sweeps(sides, ring):
    starts = []
    for (field, pairs), dst, a, q, (lo, hi) in sides:
        first, last = field[row_at(0), :], field[row_at(7), :]
        prev = jnp.where(lo, 0.0, roll(last, 32))
        field[row_at(8), :] = jnp.where(hi, 0.0, roll(first, 96))
        starts.append((prev[:M], up(first, prev), first))
    for half in range(8 // CHUNK):
        for n, ((field, pairs), (new_field, new_pairs), a, q, masks) in enumerate(sides):
            news = []
            starts[n] = advance(
                field, pairs, new_field, a, q, half * CHUNK, CHUNK, starts[n], lambda i, new: news.append(new)
            )
            new_pairs[pl.ds(half * CHUNK * ROW, CHUNK * ROW), :] = pair_sums(jnp.concatenate(news, axis=0), ring)


def k_strips(k_ref, left_ref, right_ref):
    region = lanes(8) // 32
    for z in range(NZ):
        turned = [roll(k_ref[z, pl.ds(8 * h, 8), :], 32 * h) for h in range(4)]
        left, right = turned[0], turned[0]
        for h in range(1, 4):
            left = jnp.where(region == h, turned[h], left)
            right = jnp.where(region == h - 1, turned[h], right)
        left_ref[z] = left
        right_ref[z] = right


def spread(value_of, dst, blocks, pad=True):
    def body(z, carry):
        for b in range(blocks):
            value = value_of(z, b)
            for m in range(M):
                dst[pl.ds(b * 8 * ROW + z * M + m, 8, stride=ROW), :] = value
        return carry

    lax.fori_loop(0, NZ, body, 0)


def strip_prepare(kl_ref, kr_ref, hl_ref, hr_ref, al, ql, ar, qr, kb):
    lane = lanes(8) % 32
    left, right = strip_masks()
    spread(lambda z, b: jnp.where(lane >= 22, hl_ref[z], kl_ref[z]), kb, 1)
    coefficients(kb, al, ql, left)
    spread(lambda z, b: jnp.where(lane < 10, hr_ref[z], kr_ref[z]), kb, 1)
    coefficients(kb, ar, qr, right)


def member(zh, y, c):
    return {"member": (zh * RING + lax.rem(y + RING, RING)) * 2 + c}


def here():
    i = lax.axis_index("member")
    return i // (2 * RING), lax.rem(i // 2, RING), lax.rem(i, 2)


def greet(targets, conditional=()):
    barrier = pltpu.get_barrier_semaphore()
    count = len(targets)
    for target in targets:
        pl.semaphore_signal(barrier, inc=1, device_id=target, device_id_type=MESH)
    for condition, target in conditional:
        @pl.when(condition)
        def _():
            pl.semaphore_signal(barrier, inc=1, device_id=target, device_id_type=MESH)

        count = count + jnp.where(condition, 1, 0)
    pl.semaphore_wait(barrier, count)


def copy_to(src, dst, send, recv, target):
    return pltpu.make_async_remote_copy(
        src_ref=src, dst_ref=dst, send_sem=send, recv_sem=recv, device_id=target, device_id_type=MESH
    )


def tile_links():
    t, n = lax.axis_index("tile"), lax.axis_size("tile")
    return (t > 0, {"tile": lax.rem(t + n - 1, n)}), (t < n - 1, {"tile": lax.rem(t + 1, n)})


def halo_start(to_left, to_right, from_left, from_right, send, recv):
    (has_left, left), (has_right, right) = tile_links()
    rightward = copy_to(to_right, from_left, send.at[0], recv.at[0], right)
    leftward = copy_to(to_left, from_right, send.at[1], recv.at[1], left)

    @pl.when(has_right)
    def _():
        rightward.start()

    @pl.when(has_left)
    def _():
        leftward.start()

    @pl.when(jnp.logical_not(has_left))
    def _():
        from_left[...] = jnp.zeros(from_left.shape, F32)

    @pl.when(jnp.logical_not(has_right))
    def _():
        from_right[...] = jnp.zeros(from_right.shape, F32)

    def finish():
        @pl.when(has_right)
        def _():
            rightward.wait_send()
            leftward.wait_recv()

        @pl.when(has_left)
        def _():
            leftward.wait_send()
            rightward.wait_recv()

    return finish


KINDS = {
    0: (0, 1, 0), 1: (0, 2, 0), 2: (0, -1, 0), 3: (0, -2, 0),
    4: (-2, 1, 0), 5: (-2, 2, 1), 6: (2, -1, 0), 7: (2, -2, 2),
}


def halved(ref, part):
    half = SV * NZ // 2
    return ref if part == 0 else ref.at[pl.ds(0 if part == 1 else half, half)]


def gather(grad, full, near, anti, pair, y_send, y_recv, p_send, p_recv, z_send, z_recv, local_sem, gt, between):
    zh, y, c = here()
    started = []

    def slot(side, d, core):
        return full.at[member(zh if side == 0 else 1 - zh, y + d, core)["member"]]

    def send(op):
        op.start()
        started.append(op)

    def y_copy(side, kind, source=None):
        d, to, part = KINDS[kind]
        place = halved(slot(side, d, c), part)
        return copy_to(place if source is None else source, place, y_send.at[side, kind], y_recv.at[side, kind], near[to])

    def z_copy(kind, source=None):
        d, to, part = KINDS[kind] if kind >= 0 else (0, 0, 0)
        place = halved(slot(0, d - to, c), part)
        n = max(kind - 3, 0)
        return copy_to(place if source is None else source, place, z_send.at[n], z_recv.at[n], anti)

    def p_copy(side, kind, core, source=None):
        d, to, part = KINDS[kind] if kind >= 0 else (0, 0, 0)
        place = halved(slot(side, d - to, core), part)
        n = side * 9 + kind + 1
        return copy_to(place if source is None else source, place, p_send.at[n], p_recv.at[n], pair)

    def arrivals(side, kinds):
        for kind in kinds:
            if side == 1 and kind >= 4:
                z_copy(kind).wait_recv()
            else:
                y_copy(side, kind).wait_recv()
            if side == 0 and kind in (1, 3):
                send(y_copy(0, kind + 4))
                send(y_copy(0, kind + 3))
            if side == 0 and kind >= 4:
                send(z_copy(kind))
            send(p_copy(side, kind, c))

    send(z_copy(-1, grad))
    for kind in (1, 3, 0, 2):
        send(y_copy(0, kind, grad))
    send(p_copy(0, -1, c, grad))
    mine = pltpu.make_async_copy(grad, slot(0, 0, c), local_sem)
    mine.start()
    between[0]()
    arrivals(0, (1, 3, 0, 2))
    z_copy(-1).wait_recv()
    for kind in (1, 3, 0, 2):
        send(y_copy(1, kind))
    send(p_copy(1, -1, c))
    between[1]()

    def unload(side, core, *ds):
        for d in ds:
            o = member(zh if side == 0 else 1 - zh, y + d, core)["member"]
            for sv in range(SV):
                gt[pl.ds(sv * NZ * NY + o, NZ, stride=NY), :] = full[o, pl.ds(sv * NZ, NZ), :]

    def from_pair(side, *kinds):
        for kind in kinds:
            p_copy(side, kind, 1 - c).wait_recv()

    mine.wait()
    unload(0, c, 0, 1, -1, 2, -2)
    unload(1, c, 0)
    arrivals(0, (4, 6, 5, 7))
    unload(0, c, 3, -3, 4)
    arrivals(1, (0, 2, 1, 3))
    unload(1, c, 1, -1, 2, -2)
    from_pair(0, -1, 0, 1, 2, 3)
    unload(0, 1 - c, 0, 1, -1, 2, -2)
    arrivals(1, (4, 6, 5, 7))
    unload(1, c, 3, -3, 4)
    from_pair(0, 4, 5, 6, 7)
    unload(0, 1 - c, 3, -3, 4)
    from_pair(1, -1, 0, 1, 2, 3)
    unload(1, 1 - c, 0, 1, -1, 2, -2)
    from_pair(1, 4, 5, 6, 7)
    unload(1, 1 - c, 3, -3, 4)
    for op in started:
        op.wait_send()


def selectors(owner, pick, place):
    lane, row = lanes(8), lax.broadcasted_iota(jnp.int32, (8, 128), 0)
    for y8 in range(0, NY, 8):
        picked = jnp.zeros((8, 128), F32)
        for i in range(8):
            picked = jnp.where((row == i) & (lane % NY == owner[y8 + i]), 1.0, picked)
        pick[pl.ds(y8, 8), :] = picked
    for d8 in range(0, NY, 8):
        placed = jnp.zeros((8, 128), F32)
        for y in range(NY):
            placed = jnp.where((lane % NY == y) & (row + d8 == owner[y]), 1.0, placed)
        place[pl.ds(d8, 8), :] = placed


def permuted(selector, values):
    rhs = jnp.concatenate(values, axis=1)
    high = rhs.astype(jnp.bfloat16)
    low = (rhs - high.astype(F32)).astype(jnp.bfloat16)
    out = jnp.dot(selector, jnp.concatenate([high, low], axis=0), preferred_element_type=F32)
    return out[:, :128], out[:, 128:]


def weigh(pick, pert, k_ref, state, gt):
    selector = pick[:, pl.ds(0, 2 * NY)].astype(jnp.bfloat16)

    def reorder(z, carry):
        for sv in range(0, SV, 2):
            places = [pl.ds(pl.multiple_of((sv + i) * NZ * NY + z * NY, NY), NY) for i in range(2)]
            for place, value in zip(places, permuted(selector, [gt[place, :] for place in places])):
                gt[place, :] = value
        return carry

    lax.fori_loop(0, NZ, reorder, 0, unroll=4)

    def body(z, carry, y0):
        grads = [gt[pl.ds(pl.multiple_of(sv * NZ * NY + z * NY + y0, 16), 16), :] for sv in range(SV)]
        k = k_ref[z, pl.ds(y0, 16), :]
        for m in range(M):
            total = None
            for sv in range(SV):
                term = pert[m, sv, z, pl.ds(y0, 16), :].astype(F32) * grads[sv]
                total = term if total is None else total + term
            total = total * k
            for part in range(2):
                start = (y0 + 8 * part) * ROW + z * M + m
                state[pl.ds(start, 8, stride=ROW), :] = total[8 * part : 8 * part + 8]
        return carry

    for y0 in (0, 16):
        lax.fori_loop(0, NZ, functools.partial(body, y0=y0), 0)


def cut_strips(state, pairs, vl, vr, ring):
    region = lanes(ROW) // 32

    def body(y, carry):
        quarters = [state[row_at(8 * h + y), :] for h in range(4)]
        turned = [roll(row, 32 * h) for h, row in enumerate(quarters)]
        sums = pair_sums(jnp.concatenate(quarters, axis=0), ring)
        for h in range(4):
            pairs[row_at(8 * h + y), :] = sums[h * ROW : (h + 1) * ROW]
        left, right = turned[0], turned[0]
        for h in range(1, 4):
            left = jnp.where(region == h, turned[h], left)
            right = jnp.where(region == h - 1, turned[h], right)
        rows = pl.ds(pl.multiple_of(y * ROW, ROW), ROW)
        vl[rows, :] = left
        vr[rows, :] = right
        return carry

    lax.fori_loop(0, 8, body, 0, unroll=4)


def evens(row, odd):
    return jnp.concatenate([row[M * (2 * i + odd) : M * (2 * i + odd + 1)] for i in range(4)], axis=0)


def pack_strips(vl, vr, to_left, to_right):
    lane = lanes(ROW // 2) % 32

    def body(y, carry):
        rows = pl.ds(pl.multiple_of(y * ROW, ROW), ROW)
        out = pl.ds(pl.multiple_of(y * ROW // 2, ROW // 2), ROW // 2)
        right, left = vr[rows, :], vl[rows, :]
        to_right[out, :] = jnp.where(lane >= 22, evens(right, 0), roll(evens(right, 1), 118))
        to_left[out, :] = jnp.where(lane < 10, evens(left, 0), roll(evens(left, 1), 10))
        return carry

    lax.fori_loop(0, 8, body, 0, unroll=4)


def unpack_strips(from_left, from_right, vl, vr, lp, rp, ring):
    lane = lanes(ROW) % 32

    def mixed(even, odd):
        return jnp.concatenate([part[M * i : M * i + M] for i in range(4) for part in (even, odd)], axis=0)

    def body(y, carry):
        rows = pl.ds(pl.multiple_of(y * ROW, ROW), ROW)
        packed = pl.ds(pl.multiple_of(y * ROW // 2, ROW // 2), ROW // 2)
        left, right = from_left[packed, :], from_right[packed, :]
        left = jnp.where(lane >= 22, mixed(left, roll(left, 10)), vl[rows, :])
        right = jnp.where(lane < 10, mixed(right, roll(right, 118)), vr[rows, :])
        vl[rows, :] = left
        vr[rows, :] = right
        sums = pair_sums(jnp.concatenate([left, right], axis=0), ring)
        lp[rows, :] = sums[:ROW]
        rp[rows, :] = sums[ROW:]
        return carry

    lax.fori_loop(0, 8, body, 0, unroll=4)


def merge_strips(state, vl, vr):
    lane = lanes(ROW)
    inner = (lane >= 10) & (lane < 118)

    def body(y, carry):
        rows = pl.ds(pl.multiple_of(y * ROW, ROW), ROW)
        edge = jnp.where(lane % 32 < 10, vl[rows, :], vr[rows, :])
        for h in range(4):
            place = pl.ds(pl.multiple_of((8 * h + y) * ROW, ROW), ROW)
            state[place, :] = jnp.where(inner, state[place, :], roll(edge, -32 * h))
        return carry

    lax.fori_loop(0, 8, body, 0, unroll=4)


def second_pass(pert, k_ref, state, natural, inc, place, norm):
    def body(z, carry, y0):
        factor = norm / k_ref[z, pl.ds(y0, 16), :]
        local = []
        for m in range(M):
            starts = [(y0 + 8 * part) * ROW + z * M + m for part in range(2)]
            local.append(jnp.concatenate([state[pl.ds(s, 8, stride=ROW), :] for s in starts], axis=0))
        for sv in range(SV):
            total = None
            for m in range(M):
                term = pert[m, sv, z, pl.ds(y0, 16), :].astype(F32) * local[m]
                total = term if total is None else total + term
            natural[pl.ds(pl.multiple_of(sv * NZ * NY + z * NY + y0, 16), 16), :] = total * factor
        return carry

    for y0 in (0, 16):
        lax.fori_loop(0, NZ, functools.partial(body, y0=y0), 0)
    selector = place[:, pl.ds(0, 2 * NY)].astype(jnp.bfloat16)

    def reorder(z, carry):
        for sv in range(0, SV, 2):
            values = [natural[pl.ds(pl.multiple_of((sv + i) * NZ * NY + z * NY, NY), NY), :] for i in range(2)]
            for i, value in enumerate(permuted(selector, values)):
                for d8 in range(0, NY, 8):
                    inc[pl.ds(d8 * SV * NZ + (sv + i) * NZ + z, 8, stride=SV * NZ), :] = value[d8 : d8 + 8]
        return carry

    lax.fori_loop(0, NZ, reorder, 0, unroll=4)


def reduce(inc, out, total, other, got, near, anti, pair, p_send, p_recv, send_sem, recv_sem):
    zh, y, c = here()
    started = []

    def block(side, d):
        return (zh if side == 0 else 1 - zh) * RING + lax.rem(y + d + RING, RING)

    def p_copy(n):
        b = block(*ORDER[n])
        return copy_to(inc.at[rows_of(b, 1 - c)], other.at[b], p_send.at[n], p_recv.at[n], pair)

    def send(op):
        op.start()
        started.append(op)

    def rows_of(b, core):
        return pl.ds(pl.multiple_of((2 * b + core) * SV * NZ, SV * NZ), SV * NZ)

    def to(n, side, d, target, part=0):
        return copy_to(
            halved(total.at[block(side, d)], part), halved(got.at[n], part), send_sem.at[n], recv_sem.at[n], target
        )

    def paired(side, *ds):
        for d in ds:
            n = ORDER.index((side, d))
            p_copy(n).wait_recv()
            b = block(side, d)
            total[b] = inc[rows_of(b, c), :] + other[b]

    def add(n, side, d, target, part=0):
        to(n, side, d, target, part).wait_recv()
        b = block(side, d)
        if part == 0:
            total[b] += got[n]
        else:
            half = SV * NZ // 2
            rows = pl.ds(0 if part == 1 else half, half)
            total[b, rows, :] += got[n, rows, :]

    for n in range(len(ORDER)):
        send(p_copy(n))

    for n, d in ((0, 4), (1, 3), (2, -3)):
        paired(1, d)
        send(to(n, 1, d, anti))
    for n, d in ((3, 2), (4, -2), (5, 1), (6, -1)):
        paired(1, d)
        send(to(n, 1, d, near[d]))
    paired(0, 4, 3, -3)
    for n, d in ((7, 1), (8, -1)):
        paired(0, d)
        send(to(n, 0, d, near[d]))
    paired(0, 2, -2)
    paired(1, 0)
    paired(0, 0)
    add(0, 0, 4, anti)
    send(to(9, 0, 4, near[2], 1))
    send(to(10, 0, 4, near[-2], 2))
    add(1, 0, 3, anti)
    send(to(11, 0, 3, near[1]))
    add(2, 0, -3, anti)
    send(to(12, 0, -3, near[-1]))
    for n, d in ((5, 1), (6, -1), (3, 2), (4, -2)):
        add(n, 1, 0, near[d])
    send(to(13, 1, 0, anti))
    add(9, 0, 2, near[2], 1)
    add(11, 0, 2, near[1])
    send(to(14, 0, 2, near[2]))
    add(10, 0, -2, near[-2], 2)
    add(12, 0, -2, near[-1])
    send(to(15, 0, -2, near[-2]))
    for n in (7, 8, 13, 14, 15):
        to(n, 0, 0, anti).wait_recv()
    out[...] = ((total[block(0, 0)] + got[7]) + (got[8] + got[13])) + (got[14] + got[15])
    for op in started:
        op.wait_send()


ORDER = (
    (1, 4), (1, 3), (1, -3), (1, 2), (1, -2), (1, 1), (1, -1), (0, 4), (0, 3), (0, -3), (0, 1), (0, -1),
    (0, 2), (0, -2), (1, 0), (0, 0),
)


def kernel(owner, grad, k_ref, pert_in, out, *scratch, norm, names):
    r = dict(zip(names, scratch))
    zh, y, c = here()
    near = {d: member(zh, y + d, c) for d in (1, 2, -1, -2)}
    anti, pair = member(1 - zh, y, c), member(zh, y, 1 - c)
    pert, s0, s1, l0, l1, r0, r1 = (r[n] for n in ("pert", "s0", "s1", "l0", "l1", "r0", "r1"))
    fetch = pltpu.make_async_copy(pert_in, pert, r["pert_sem"])
    fetch.start()
    greet(list(near.values()) + [anti, pair], tile_links())
    left, right = strip_masks()
    kb, halos = r["kb"], []

    def first():
        ring_matrix(r["ring"])
        k_strips(k_ref, r["kl"], r["kr"])
        halos.append(halo_start(r["kl"], r["kr"], r["hl"], r["hr"], r["h_send"], r["h_recv"]))
        kb[row_at(NY), :] = jnp.zeros((ROW, 128), F32)
        s0[row_at(NY), :] = jnp.zeros((ROW, 128), F32)
        s1[row_at(NY), :] = jnp.zeros((ROW, 128), F32)
        spread(lambda z, b: k_ref[z, pl.ds(8 * b, 8), :], kb, 4)
        coefficients(kb, r["a"], r["q"])

    def second():
        selectors(owner, r["pick"], r["place"])
        halos[0]()
        strip_prepare(r["kl"], r["kr"], r["hl"], r["hr"], r["al"], r["ql"], r["ar"], r["qr"], kb)

    gather(
        grad, r["full"], near, anti, pair, r["y_send"], r["y_recv"], r["p_send"], r["p_recv"], r["z_send"], r["z_recv"],
        r["local_sem"], r["gt"], (first, second),
    )
    fetch.wait()
    weigh(r["pick"], pert, k_ref, s0, r["gt"])
    cut_strips(s0, r["sp0"], l0, r0, r["ring"])
    pack_strips(l0, r0, r["to_left"], r["to_right"])
    finish = halo_start(r["to_left"], r["to_right"], r["from_left"], r["from_right"], r["s_send"], r["s_recv"])

    main = ((s0, r["sp0"]), (s1, r["sp1"]))
    lefts = ((l0, r["lp0"]), (l1, r["lp1"]))
    rights = ((r0, r["rp0"]), (r1, r["rp1"]))

    def two_main(i, carry):
        for n in range(2):
            main_sweep(main[n], main[1 - n], r["a"], r["q"], r["ring"])
        return carry

    def two_strips(i, carry):
        for n in range(2):
            strip_sweeps(
                ((lefts[n], lefts[1 - n], r["al"], r["ql"], left), (rights[n], rights[1 - n], r["ar"], r["qr"], right)),
                r["ring"],
            )
        return carry

    lax.fori_loop(0, SWEEPS // 2, two_main, 0)
    finish()
    unpack_strips(r["from_left"], r["from_right"], l0, r0, r["lp0"], r["rp0"], r["ring"])
    lax.fori_loop(0, SWEEPS // 2, two_strips, 0)
    merge_strips(s0, l0, r0)
    second_pass(pert, k_ref, s0, r["gt"], r["inc"], r["place"], norm)
    reduce(
        r["inc"], out, r["total"], r["other"], r["got"], near, anti, pair,
        r["rp_send"], r["rp_recv"], r["r_send"], r["r_recv"],
    )


def body(perturbations, gradient_store, diffusivity, slab_owner):
    members = perturbations.shape[0] * lax.axis_size("member")
    pert = perturbations.reshape(M, SV, NZ, NY, 128)
    grad = gradient_store.reshape(SV * NZ, 128)
    dma = pltpu.SemaphoreType.DMA

    def f32(*shape):
        return pltpu.VMEM(shape + (128,), F32)

    scratch = {
        "pert": pltpu.VMEM(pert.shape, pert.dtype), "pert_sem": dma,
        "full": f32(4 * RING, SV * NZ), "gt": f32(SV * NZ * NY), "pick": f32(NY), "place": f32(NY),
        "s0": f32((NY + 1) * ROW), "s1": f32((NY + 1) * ROW), "kb": f32((NY + 1) * ROW),
        **{n: f32(NY * ROW) for n in ("a", "q", "sp0", "sp1")},
        "ring": pltpu.VMEM((256, 128), jnp.bfloat16),
        **{n: f32(9 * ROW) for n in ("l0", "l1", "r0", "r1")},
        **{n: f32(8 * ROW) for n in ("al", "ql", "ar", "qr", "lp0", "lp1", "rp0", "rp1")},
        **{n: f32(NZ, 8) for n in ("kl", "kr", "hl", "hr")},
        **{n: f32(4 * ROW) for n in ("to_left", "to_right", "from_left", "from_right")},
        "inc": f32(NY * SV * NZ),
        **{n: f32(2 * RING, SV * NZ) for n in ("total", "other", "got")},
        **{n: dma((2, 8)) for n in ("y_send", "y_recv")},
        **{n: dma((18,)) for n in ("p_send", "p_recv")},
        **{n: dma((5,)) for n in ("z_send", "z_recv")},
        "local_sem": dma,
        **{n: dma((2,)) for n in ("h_send", "h_recv", "s_send", "s_recv")},
        **{n: dma((16,)) for n in ("rp_send", "rp_recv", "r_send", "r_recv")},
    }
    out = pl.pallas_call(
        functools.partial(kernel, norm=1.0 / (members - 1), names=tuple(scratch)),
        out_shape=jax.ShapeDtypeStruct((SV * NZ, 128), F32),
        in_specs=[SMEM, VMEM, VMEM, pl.BlockSpec(memory_space=pl.ANY)],
        out_specs=VMEM,
        scratch_shapes=list(scratch.values()),
        compiler_params=pltpu.CompilerParams(vmem_limit_bytes=LIMIT, collective_id=0, has_side_effects=True),
    )(slab_owner, grad, diffusivity, pert)
    return out.reshape(gradient_store.shape)


def solution(mesh):
    in_specs = (
        P("member", None, None, None, None, "tile"),
        P(None, None, None, "member", "tile"),
        P(None, None, "tile"),
        P(),
    )
    out_specs = P(None, None, None, "member", "tile")
    return jax.shard_map(body, mesh=mesh, in_specs=in_specs, out_specs=out_specs, check_vma=False)
```
